32 devices in a mesh: shard: 8 (over z, x), head: 2 (over core), tensor: 2 (over y).
Axes of the slice: x: 2, y: 2, z: 4, core: 2. Of those that a mesh axis runs over, the one named last changes fastest.
Arguments:
- tokens: bfloat16 [64, 320, 1024], P('shard'), may hold values from -6 to 6
- kept_counts: int32 [64], P('shard'), may hold values from 200 to 256
- cotangent: bfloat16 [64, 320, 1024], P(('shard', 'head')), may hold values from -6 to 6
- w_qkv: bfloat16 [3, 1024, 1024], P(None, 'shard', 'head'), may hold values from -0.1875 to 0.1875
- w_out: bfloat16 [1024, 1024], P('head', 'shard'), may hold values from -1.5 to 1.5
- w_up: bfloat16 [1024, 4096], P('shard', 'tensor'), may hold values from -0.1875 to 0.1875
- w_down: bfloat16 [4096, 1024], P('tensor', 'shard'), may hold values from -0.09375 to 0.09375
- ln1_gain: float32 [1024], replicated, may hold values from 0.5 to 1.5
- ln1_bias: float32 [1024], replicated, may hold values from -1.5 to 1.5
- ln2_gain: float32 [1024], replicated, may hold values from 0.5 to 1.5
- ln2_bias: float32 [1024], replicated, may hold values from -1.5 to 1.5
- out_bias: float32 [1024], replicated, may hold values from -1.5 to 1.5
- up_bias: float32 [4096], replicated, may hold values from -2.5 to 2.5
- down_bias: float32 [1024], replicated, may hold values from -1.5 to 1.5
- attn_owner: int32 [2, 512, 1], P('head'), may hold values from 0 to 15; in each aligned block of 512 rows (0 to 511, 512 to 1023, ..., all dimensions but the last counted through in order) at most 33 rows name the same one
- mlp_owner: int32 [2, 1024, 1], P('tensor'), may hold values from 0 to 15; in each aligned block of 1024 rows (0 to 1023, 1024 to 2047, ..., all dimensions but the last counted through in order) at most 65 rows name the same one
- attn_left: float32 [2, 528, 64, 64], P('head', ('shard', 'tensor')), may hold values from -0.75 to 0.75
- attn_right: float32 [2, 528, 64, 64], P('head', ('shard', 'tensor')), may hold values from -0.75 to 0.75
- attn_first: float32 [2, 528, 64, 64], P('head', ('shard', 'tensor')), may hold values from -16 to 16
- attn_second: float32 [2, 528, 64, 64], P('head', ('shard', 'tensor')), may hold values from 40.96 to 614.4
- attn_master: float32 [2, 528, 64, 64], P('head', ('shard', 'tensor')), may hold values from -0.1875 to 0.1875
- mlp_left: float32 [2, 1040, 64, 64], P('tensor', ('shard', 'head')), may hold values from -0.75 to 0.75
- mlp_right: float32 [2, 1040, 64, 64], P('tensor', ('shard', 'head')), may hold values from -0.75 to 0.75
- mlp_first: float32 [2, 1040, 64, 64], P('tensor', ('shard', 'head')), may hold values from -16 to 16
- mlp_second: float32 [2, 1040, 64, 64], P('tensor', ('shard', 'head')), may hold values from 40.96 to 614.4
- mlp_master: float32 [2, 1040, 64, 64], P('tensor', ('shard', 'head')), may hold values from -0.1875 to 0.1875
Outputs:
- out: bfloat16 [64, 320, 1024], P(('shard', 'head', 'tensor'))
- tokens_grad: float32 [64, 320, 1024], P(('shard', 'head', 'tensor'))
- ln1_gain_grad: float32 [1024], replicated
- ln1_bias_grad: float32 [1024], replicated
- ln2_gain_grad: float32 [1024], replicated
- ln2_bias_grad: float32 [1024], replicated
- out_bias_grad: float32 [1024], replicated
- down_bias_grad: float32 [1024], replicated
- up_bias_grad: float32 [4096], replicated
- attn_grad: float32 [2, 528, 64, 64], P('head', ('shard', 'tensor'))
- attn_first_new: float32 [2, 528, 64, 64], P('head', ('shard', 'tensor'))
- attn_second_new: float32 [2, 528, 64, 64], P('head', ('shard', 'tensor'))
- attn_master_new: float32 [2, 528, 64, 64], P('head', ('shard', 'tensor'))
- mlp_grad: float32 [2, 1040, 64, 64], P('tensor', ('shard', 'head'))
- mlp_first_new: float32 [2, 1040, 64, 64], P('tensor', ('shard', 'head'))
- mlp_second_new: float32 [2, 1040, 64, 64], P('tensor', ('shard', 'head'))
- mlp_master_new: float32 [2, 1040, 64, 64], P('tensor', ('shard', 'head'))
- w_qkv_new: bfloat16 [3, 1024, 1024], P(None, 'shard', 'head')
- w_out_new: bfloat16 [1024, 1024], P('head', 'shard')
- w_up_new: bfloat16 [1024, 4096], P('shard', 'tensor')
- w_down_new: bfloat16 [4096, 1024], P('tensor', 'shard')
The draws below stay inside these ranges and needn't reach their ends.
Inputs may be any that keep to these rules, and one draw needn't show every extreme that they name: `attn_owner`: the owner of each block, an index along shard and tensor; no owner holds more than 33 blocks of one head group, and some owner holds exactly 33. `mlp_owner`: the owner of each block, an index along shard and head; no owner holds more than 65 blocks of one hidden-unit group, and some owner holds exactly 65.
All inputs are finite; a program needn't handle non-finite values.
Results may differ from the reference program's by a relative error of at most 0.015.
Values may be sent and summed in bfloat16 or wider, within the bound.
No kernel may reach another device: no remote copies, remote signals or barrier semaphores. Data moves between devices by JAX's collectives and lax.ppermute only.
A program may use at most 256 MiB of HBM per device.

```python
import math
from functools import partial
import jax
import jax.numpy as jnp
import numpy as np
from jax import lax

D = 1024
HEADS = 16
HD = 64
FF = 4096
BUF = 64
KEPT_MAX = 256
SLOTS = 320
BS = 64
IMAGES = 64
OWN_A = 16
OWN_M = 16
BLK_A = 512
BLK_M = 1024
CAP_A = 33
CAP_M = 65
N_HEAD = 2
N_TENSOR = 2


def place_ends(values, own_key, low, high):
    index_at = [jax.random.randint(jax.random.fold_in(own_key, axis), (), 0, length) for axis, length in enumerate(values.shape)]
    main_axis = values.shape.index(max(values.shape))
    neighbour = index_at[:main_axis] + [(index_at[main_axis] + 1) % values.shape[main_axis]] + index_at[main_axis + 1:]
    return values.at[tuple(index_at)].set(low).at[tuple(neighbour)].set(high)


def steps_of(rng, shape, shards, low, largest):
    level, own = 1.0, jax.random.fold_in(rng, 6)
    for dim, shards_of in shards:
        draws = jnp.exp(jax.random.uniform(jax.random.fold_in(own, dim), (shards_of,), jnp.float32, low / len(shards), largest / len(shards)))
        level = level * jnp.repeat(draws, shape[dim] // shards_of).reshape([-1 if axis == dim else 1 for axis in range(len(shape))])
    return level


def routed_block(stream_key, own, number, rows, count, top, bound, lean):
    ranking = jax.random.permutation(stream_key, count)
    crowded, ordinary = shares(count, rows * top, bound, lean, True), shares(count, rows * top, bound, lean, False)
    places = jnp.arange(count)

    def named(lengths, turn):
        used = int((lengths > 0).sum())
        fixed = max(1, used // 4)
        shifted = fixed + (places - fixed + turn * (used - fixed)) % max(1, count - fixed)
        return jnp.zeros((count,), jnp.int32).at[ranking[jnp.where(places < fixed, places, shifted)]].set(jnp.asarray(lengths, jnp.int32))

    lengths = jnp.where(number % 4 == 0, named(crowded, number // 4), named(ordinary, number - number // 4 - 1))
    mixed = jax.random.permutation(jax.random.fold_in(own, 3), count)
    source_of, sink = mixed[0:count // 2 * 2:2], mixed[1:count // 2 * 2:2]
    room = jnp.minimum(lengths[source_of] - 1, bound - lengths[sink]) // 2
    room = jnp.where((source_of == ranking[0]) | (sink == ranking[0]) | (lengths[sink] == 0), 0, jnp.maximum(room, 0))
    shifted = jax.random.randint(jax.random.fold_in(own, 4), (count // 2,), 0, 1 << 20) % (room + 1)
    lengths = lengths.at[source_of].add(-shifted).at[sink].add(shifted)
    members = jnp.searchsorted(jnp.cumsum(lengths), jnp.arange(rows * top), side="right").astype(jnp.int32)
    grid = members.reshape(top, rows).T
    grid = grid[jax.random.permutation(jax.random.fold_in(own, 1), rows)]
    turn = jax.random.randint(jax.random.fold_in(own, 2), (rows, 1), 0, top)
    return jnp.take_along_axis(grid, (jnp.arange(top)[None, :] + turn) % top, axis=1)


def shares(amount, total, limit, skew, full):
    weights = [(1 << 20) // math.isqrt(standing ** skew) + 1 for standing in range(1, amount + 1)]
    largest = limit if full else min(limit, max(-(-total // amount), total * weights[0] // sum(weights)))
    least = 1 if total - largest >= amount - 1 else 0
    given, rest = [largest] + [least] * (amount - 1), total - largest - least * (amount - 1)
    while rest > 0:
        movable = [i for i in range(1, amount) if given[i] < largest] or [i for i in range(1, amount) if given[i] < limit]
        pool, left = sum([weights[i] for i in movable]), rest
        for i in movable:
            addition = min(limit - given[i], max(1, left * weights[i] // pool), rest)
            given[i] = given[i] + addition
            rest = rest - addition
    return np.array(given)


def gaussian(rng, dims, spread, most, split=(), held_as=jnp.bfloat16):
    values = spread * jax.random.normal(rng, dims, jnp.float32)
    if split:
        values = values * steps_of(rng, dims, split, -0.22, 0.18)
    return jnp.clip(values, -most, most).astype(held_as)


def setup_inputs(seed: int = 0) -> dict:
    key_list = jax.random.split(jax.random.key(seed), 27)
    tokens = gaussian(key_list[0], (IMAGES, SLOTS, D), 1.0, 6.0, ((0, 8),))
    kept_counts = place_ends(jax.random.randint(key_list[1], (IMAGES,), KEPT_MAX * 25 // 32, KEPT_MAX + 1), jax.random.fold_in(key_list[1], 1), KEPT_MAX * 25 // 32, KEPT_MAX).astype(jnp.int32)
    cotangent = gaussian(key_list[2], (IMAGES, SLOTS, D), 1.0, 6.0, ((0, 16),))
    w_qkv = gaussian(key_list[3], (3, D, D), D ** -0.5, 0.1875, ((1, 8), (2, 2)))
    w_out = gaussian(key_list[4], (D, D), (D // 64) ** -0.5, 1.5, ((0, 2), (1, 8)))
    w_up = gaussian(key_list[5], (D, FF), D ** -0.5, 0.1875, ((0, 8), (1, 2)))
    w_down = gaussian(key_list[6], (FF, D), FF ** -0.5, 0.09375, ((0, 2), (1, 8)))
    ln1_gain = jnp.clip(1.0 + 0.1 * jax.random.normal(key_list[7], (D,), jnp.float32), 0.5, 1.5)
    ln1_bias = gaussian(key_list[8], (D,), 0.3, 1.5, (), jnp.float32)
    ln2_gain = jnp.clip(1.0 + 0.1 * jax.random.normal(key_list[9], (D,), jnp.float32), 0.5, 1.5)
    ln2_bias = gaussian(key_list[10], (D,), 0.3, 1.5, (), jnp.float32)
    out_bias = gaussian(key_list[11], (D,), 0.3, 1.5, (), jnp.float32)
    up_bias = gaussian(key_list[12], (FF,), 0.5, 2.5, (), jnp.float32)
    down_bias = gaussian(key_list[13], (D,), 0.3, 1.5, (), jnp.float32)
    attn_owner_keys = jax.random.split(jax.random.fold_in(key_list[14], 1), N_HEAD * BLK_A // BLK_A)
    attn_owner_turns = jax.random.permutation(jax.random.fold_in(key_list[14], 3), N_HEAD * BLK_A // BLK_A)
    attn_owner = jax.vmap(lambda own, number: routed_block(jax.random.fold_in(key_list[14], 2), own, number, BLK_A, OWN_A, 1, CAP_A, 2))(attn_owner_keys, attn_owner_turns).reshape((N_HEAD, BLK_A, 1))
    mlp_owner_keys = jax.random.split(jax.random.fold_in(key_list[15], 1), N_TENSOR * BLK_M // BLK_M)
    mlp_owner_turns = jax.random.permutation(jax.random.fold_in(key_list[15], 3), N_TENSOR * BLK_M // BLK_M)
    mlp_owner = jax.vmap(lambda own, number: routed_block(jax.random.fold_in(key_list[15], 2), own, number, BLK_M, OWN_M, 1, CAP_M, 2))(mlp_owner_keys, mlp_owner_turns).reshape((N_TENSOR, BLK_M, 1))
    attn_left = gaussian(key_list[16], (N_HEAD, OWN_A * CAP_A, BS, BS), BS ** -0.5, 0.75, ((0, 2), (1, 16)), jnp.float32)
    attn_right = gaussian(key_list[17], (N_HEAD, OWN_A * CAP_A, BS, BS), BS ** -0.5, 0.75, ((0, 2), (1, 16)), jnp.float32)
    attn_first = gaussian(key_list[18], (N_HEAD, OWN_A * CAP_A, BS, BS), (0.02 * (IMAGES * SLOTS) ** 0.5), 16.0, ((0, 2), (1, 16)), jnp.float32)
    attn_second = jnp.clip(jnp.exp(math.log(614.4) - 2.7080503 * jax.random.uniform(key_list[19], (N_HEAD, OWN_A * CAP_A, BS, BS), jnp.float32) ** steps_of(key_list[19], (N_HEAD, OWN_A * CAP_A, BS, BS), ((0, 2), (1, 16)), -0.2, 0.2)), 40.96, 614.4)
    attn_master = gaussian(key_list[20], (N_HEAD, OWN_A * CAP_A, BS, BS), D ** -0.5, 0.1875, ((0, 2), (1, 16)), jnp.float32)
    mlp_left = gaussian(key_list[21], (N_TENSOR, OWN_M * CAP_M, BS, BS), BS ** -0.5, 0.75, ((0, 2), (1, 16)), jnp.float32)
    mlp_right = gaussian(key_list[22], (N_TENSOR, OWN_M * CAP_M, BS, BS), BS ** -0.5, 0.75, ((0, 2), (1, 16)), jnp.float32)
    mlp_first = gaussian(key_list[23], (N_TENSOR, OWN_M * CAP_M, BS, BS), (0.02 * (IMAGES * SLOTS) ** 0.5), 16.0, ((0, 2), (1, 16)), jnp.float32)
    mlp_second = jnp.clip(jnp.exp(math.log(614.4) - 2.7080503 * jax.random.uniform(key_list[24], (N_TENSOR, OWN_M * CAP_M, BS, BS), jnp.float32) ** steps_of(key_list[24], (N_TENSOR, OWN_M * CAP_M, BS, BS), ((0, 2), (1, 16)), -0.2, 0.2)), 40.96, 614.4)
    mlp_master = gaussian(key_list[25], (N_TENSOR, OWN_M * CAP_M, BS, BS), D ** -0.5, 0.1875, ((0, 2), (1, 16)), jnp.float32)
    return dict(tokens=tokens, kept_counts=kept_counts, cotangent=cotangent, w_qkv=w_qkv, w_out=w_out, w_up=w_up, w_down=w_down, ln1_gain=ln1_gain, ln1_bias=ln1_bias, ln2_gain=ln2_gain, ln2_bias=ln2_bias, out_bias=out_bias, up_bias=up_bias, down_bias=down_bias, attn_owner=attn_owner, mlp_owner=mlp_owner, attn_left=attn_left, attn_right=attn_right, attn_first=attn_first, attn_second=attn_second, attn_master=attn_master, mlp_left=mlp_left, mlp_right=mlp_right, mlp_first=mlp_first, mlp_second=mlp_second, mlp_master=mlp_master)


@jax.custom_vjp
def low(v):
    return lax.optimization_barrier(v.astype(jnp.bfloat16)).astype(jnp.float32)

@jax.custom_vjp
def low_back(v):
    return v

def low_keep(v):
    return (low(v), None)

def low_pass(kept, grad):
    return (grad,)

def back_keep(v):
    return (v, None)

def back_low(kept, grad):
    return (low(grad),)
low.defvjp(low_keep, low_pass)
low_back.defvjp(back_keep, back_low)
precise = lax.Precision.HIGHEST

def both_ways(value):
    return low_back(low(value))

def layer_norm(value, gain_vec, shift_vec):
    center = value - lax.optimization_barrier(jnp.mean(value, axis=-1, keepdims=True))
    inv_root = lax.rsqrt(lax.optimization_barrier(jnp.mean(center * center, axis=-1, keepdims=True)) + 1e-06)
    return center * inv_root * gain_vec + shift_vec

def group_forward(params, pieces):
    w_qkv, w_out, w_up, w_down, ln1_gain, ln1_bias, ln2_gain, ln2_bias, out_bias, up_bias, down_bias = params
    images, kept_counts = pieces
    img_count = images.shape[0]
    slot_ids = jnp.arange(SLOTS, dtype=jnp.int32)
    valid_mask = slot_ids[None, :] < (BUF + kept_counts)[:, None]
    normed_one = low(layer_norm(images, ln1_gain, ln1_bias))
    projected = both_ways(jnp.einsum('nsd,cde->cnse', normed_one, w_qkv, precision=precise))
    queries = projected[0].reshape(img_count, SLOTS, HEADS, HD)
    key_rows = projected[1].reshape(img_count, SLOTS, HEADS, HD)
    value_rows = projected[2].reshape(img_count, SLOTS, HEADS, HD)
    scores = jnp.einsum('nqhe,nkhe->nhqk', queries, key_rows, precision=precise) * 0.125
    scores = low_back(jnp.where(valid_mask[:, None, None, :], scores, -1000000000.0))
    attn_probs = low(jax.nn.softmax(scores, axis=-1))
    heads_out = jnp.einsum('nhqk,nkhe->nqhe', attn_probs, value_rows, precision=precise)
    heads_out = both_ways(heads_out.reshape(img_count, SLOTS, D))
    branch = low_back(jnp.einsum('nse,ed->nsd', heads_out, w_out, precision=precise) + out_bias)
    residual = images + branch
    normed_two = low(layer_norm(residual, ln2_gain, ln2_bias))
    pre_act = low_back(jnp.einsum('nsd,df->nsf', normed_two, w_up, precision=precise) + up_bias)
    hidden = low(jax.nn.gelu(pre_act, approximate=False))
    mlp_out = low_back(jnp.einsum('nsf,fd->nsd', hidden, w_down, precision=precise) + down_bias)
    return valid_mask[:, :, None].astype(images.dtype) * (residual + mlp_out)

def slot_numbers(owner_list, capacity, owners):
    onehot = (owner_list[:, None] == jnp.arange(owners, dtype=jnp.int32)[None, :]).astype(jnp.int32)
    earlier = jnp.cumsum(onehot, axis=0) - onehot
    return owner_list * capacity + lax.optimization_barrier(jnp.sum(earlier * onehot, axis=1))

def place_slots(blocks_in, slot_ids, total):
    return jnp.zeros((total,) + blocks_in.shape[1:], blocks_in.dtype).at[slot_ids].set(blocks_in)

def attn_split(grad_qkv, grad_out):
    group_cols = D // N_HEAD
    qkv_part = grad_qkv.reshape(3, D // BS, BS, N_HEAD, group_cols // BS, BS).transpose(3, 0, 1, 4, 2, 5)
    qkv_part = qkv_part.reshape(N_HEAD, -1, BS, BS)
    out_part = grad_out.reshape(N_HEAD, group_cols // BS, BS, D // BS, BS).transpose(0, 1, 3, 2, 4)
    out_part = out_part.reshape(N_HEAD, -1, BS, BS)
    return jnp.concatenate([qkv_part, out_part], axis=1)

def attn_join(blocks_in):
    group_cols = D // N_HEAD
    qkv_count = 3 * (D // BS) * (group_cols // BS)
    qkv_part = blocks_in[:, :qkv_count].reshape(N_HEAD, 3, D // BS, group_cols // BS, BS, BS)
    qkv_part = qkv_part.transpose(1, 2, 4, 0, 3, 5).reshape(3, D, D)
    out_part = blocks_in[:, qkv_count:].reshape(N_HEAD, group_cols // BS, D // BS, BS, BS)
    out_part = out_part.transpose(0, 1, 3, 2, 4).reshape(D, D)
    return (qkv_part, out_part)

def mlp_split(grad_up, grad_down):
    hidden_cols = FF // N_TENSOR
    up_part = grad_up.reshape(D // BS, BS, N_TENSOR, hidden_cols // BS, BS).transpose(2, 0, 3, 1, 4)
    up_part = up_part.reshape(N_TENSOR, -1, BS, BS)
    down_part = grad_down.reshape(N_TENSOR, hidden_cols // BS, BS, D // BS, BS).transpose(0, 1, 3, 2, 4)
    down_part = down_part.reshape(N_TENSOR, -1, BS, BS)
    return jnp.concatenate([up_part, down_part], axis=1)

def mlp_join(blocks_in):
    hidden_cols = FF // N_TENSOR
    up_count = D // BS * (hidden_cols // BS)
    up_part = blocks_in[:, :up_count].reshape(N_TENSOR, D // BS, hidden_cols // BS, BS, BS)
    up_part = up_part.transpose(1, 3, 0, 2, 4).reshape(D, FF)
    down_part = blocks_in[:, up_count:].reshape(N_TENSOR, hidden_cols // BS, D // BS, BS, BS)
    down_part = down_part.transpose(0, 1, 3, 2, 4).reshape(FF, D)
    return (up_part, down_part)

def soap_update(gradient, left_basis, right_basis, first_moment, second, master):
    turned = jnp.einsum('...ji,...jk->...ik', left_basis, gradient, precision=precise)
    turned = jnp.einsum('...ik,...kl->...il', turned, right_basis, precision=precise)
    first_new = 0.95 * first_moment + 0.05 * turned
    second_new = 0.95 * second + 0.05 * turned * turned
    direction = first_new / (jnp.sqrt(second_new) + 1e-08)
    rotated_back = jnp.einsum('...ij,...jk->...ik', left_basis, direction, precision=precise)
    rotated_back = jnp.einsum('...ik,...lk->...il', rotated_back, right_basis, precision=precise)
    return (first_new, second_new, master - 0.05 * rotated_back)

def reference(tokens, kept_counts, cotangent, w_qkv, w_out, w_up, w_down, ln1_gain, ln1_bias, ln2_gain, ln2_bias, out_bias, up_bias, down_bias, attn_owner, mlp_owner, attn_left, attn_right, attn_first, attn_second, attn_master, mlp_left, mlp_right, mlp_first, mlp_second, mlp_master):
    params = tuple((array_in.astype(jnp.float32) for array_in in (w_qkv, w_out, w_up, w_down, ln1_gain, ln1_bias, ln2_gain, ln2_bias, out_bias, up_bias, down_bias)))
    group_images = 4
    checked = jax.checkpoint(group_forward)

    def run_all(inputs, weights_all):
        shaped = inputs.reshape(IMAGES // group_images, group_images, SLOTS, D)
        counts = kept_counts.reshape(IMAGES // group_images, group_images)

        def scan_step(carried, pieces):
            return (carried, checked(weights_all, pieces))
        _, result = lax.scan(scan_step, jnp.zeros((), jnp.float32), (shaped, counts))
        return result.reshape(IMAGES, SLOTS, D)
    result, pullback = jax.vjp(run_all, tokens.astype(jnp.float32), params)
    tokens_grad, gradients = pullback(cotangent.astype(jnp.float32))
    g_qkv, g_out, g_up, g_down, g_ln1_gain, g_ln1_bias, g_ln2_gain, g_ln2_bias, g_out_bias, g_up_bias, g_down_bias = gradients
    attn_slot_ids = jax.vmap(lambda owner_row: slot_numbers(owner_row, CAP_A, OWN_A))(attn_owner[:, :, 0])
    attn_grad = jax.vmap(partial(place_slots, total=OWN_A * CAP_A))(attn_split(g_qkv, g_out), attn_slot_ids)
    attn_first_new, attn_second_new, attn_master_new = soap_update(attn_grad, attn_left, attn_right, attn_first, attn_second, attn_master)
    attn_taken = jax.vmap(lambda masters, slot_list: jnp.take(masters, slot_list, axis=0))(attn_master_new, attn_slot_ids)
    w_qkv_new, w_out_new = attn_join(attn_taken)
    mlp_slot_ids = jax.vmap(lambda owner_row: slot_numbers(owner_row, CAP_M, OWN_M))(mlp_owner[:, :, 0])
    mlp_grad = jax.vmap(partial(place_slots, total=OWN_M * CAP_M))(mlp_split(g_up, g_down), mlp_slot_ids)
    mlp_first_new, mlp_second_new, mlp_master_new = soap_update(mlp_grad, mlp_left, mlp_right, mlp_first, mlp_second, mlp_master)
    mlp_taken = jax.vmap(lambda masters, slot_list: jnp.take(masters, slot_list, axis=0))(mlp_master_new, mlp_slot_ids)
    w_up_new, w_down_new = mlp_join(mlp_taken)
    return (result.astype(jnp.bfloat16), tokens_grad, g_ln1_gain, g_ln1_bias, g_ln2_gain, g_ln2_bias, g_out_bias, g_down_bias, g_up_bias, attn_grad, attn_first_new, attn_second_new, attn_master_new, mlp_grad, mlp_first_new, mlp_second_new, mlp_master_new, w_qkv_new.astype(jnp.bfloat16), w_out_new.astype(jnp.bfloat16), w_up_new.astype(jnp.bfloat16), w_down_new.astype(jnp.bfloat16))
```

```python
from functools import partial

import jax
import jax.numpy as jnp
from jax import lax
from jax.experimental import pallas as pl
from jax.experimental.pallas import tpu as pltpu
from jax.sharding import PartitionSpec as P

HD = 64
FF = 4096
BUF = 64
BS = 64
LANES = 128
F32 = jnp.float32
BF16 = jnp.bfloat16

precise = lax.Precision.HIGHEST


def swap(value, axis):
    return lax.ppermute(value, axis, [(0, 1), (1, 0)])


def total_over_mesh(value):
    for axis in ("head", "tensor", "shard"):
        size = lax.axis_size(axis)
        bit = 1
        while bit < size:
            partner = lax.ppermute(value, axis, [(i, i ^ bit) for i in range(size)])
            value = value + partner
            bit *= 2
    return value


def dot(left, right, contract):
    return lax.dot_general(left, right, ((contract[:1], contract[1:]), ((), ())), preferred_element_type=F32)


def norm_parts(value):
    center = value - jnp.mean(value, axis=-1, keepdims=True)
    inv_root = lax.rsqrt(jnp.mean(center * center, axis=-1, keepdims=True) + 1e-06)
    return (center * inv_root, inv_root)


def norm_back(grad_out, normed, inv_root, gain_vec):
    grad_normed = grad_out * gain_vec
    first_mean = jnp.mean(grad_normed, axis=-1, keepdims=True)
    second_mean = jnp.mean(grad_normed * normed, axis=-1, keepdims=True)
    grad_in = inv_root * (grad_normed - first_mean - normed * second_mean)
    return (grad_in, jnp.sum(grad_out * normed, axis=0), jnp.sum(grad_out, axis=0))


def masked_scores(rows, head, kept_valid, groups):
    q = rows[:, head * HD : (head + 1) * HD]
    k = rows[:, (groups + head) * HD : (groups + head + 1) * HD]
    scores = dot(q, k, (1, 1)) * 0.125
    return jnp.where(kept_valid, scores, -1000000000.0)


def soft(scores):
    shifted = jnp.exp(scores - jnp.max(scores, axis=-1, keepdims=True))
    return shifted * (1.0 / jnp.sum(shifted, axis=-1, keepdims=True))


def attn_forward_body(kept, rows, out):
    groups = rows.shape[1] // (3 * HD)
    slots = rows.shape[0]
    valid = lax.broadcasted_iota(jnp.int32, (slots, slots), 1) < BUF + kept[pl.program_id(0)]
    for pair in range(groups // 2):
        halves = []
        for head in (2 * pair, 2 * pair + 1):
            probs = soft(masked_scores(rows, head, valid, groups)).astype(BF16)
            v = rows[:, (2 * groups + head) * HD : (2 * groups + head + 1) * HD]
            halves.append(dot(probs, v, (1, 0)).astype(BF16))
        out[:, pair * LANES : (pair + 1) * LANES] = jnp.concatenate(halves, axis=1)


def attn_forward(kept, rows, slots):
    images = kept.shape[0]
    width = rows.shape[1]
    return pl.pallas_call(
        attn_forward_body,
        out_shape=jax.ShapeDtypeStruct((images * slots, width // 3), BF16),
        grid_spec=pltpu.PrefetchScalarGridSpec(
            num_scalar_prefetch=1,
            grid=(images,),
            in_specs=[pl.BlockSpec((slots, width), lambda i, kept: (i, 0))],
            out_specs=pl.BlockSpec((slots, width // 3), lambda i, kept: (i, 0)),
        ),
        name="attn_forward",
    )(kept, rows)


def attn_backward_body(kept, rows, grads, out):
    groups = rows.shape[1] // (3 * HD)
    slots = rows.shape[0]
    valid = lax.broadcasted_iota(jnp.int32, (slots, slots), 1) < BUF + kept[pl.program_id(0)]
    for pair in range(groups // 2):
        parts = ([], [], [])
        for head in (2 * pair, 2 * pair + 1):
            probs = soft(masked_scores(rows, head, valid, groups))
            q = rows[:, head * HD : (head + 1) * HD]
            k = rows[:, (groups + head) * HD : (groups + head + 1) * HD]
            v = rows[:, (2 * groups + head) * HD : (2 * groups + head + 1) * HD]
            g = grads[:, head * HD : (head + 1) * HD]
            grad_probs = dot(g, v, (1, 1))
            inner = jnp.sum(probs * grad_probs, axis=-1, keepdims=True)
            grad_scores = (probs * (grad_probs - inner)).astype(BF16)
            parts[0].append((dot(grad_scores, k, (1, 0)) * 0.125).astype(BF16))
            parts[1].append((dot(grad_scores, q, (0, 0)) * 0.125).astype(BF16))
            parts[2].append(dot(probs.astype(BF16), g, (0, 0)).astype(BF16))
        for which in range(3):
            start = which * groups * HD + pair * LANES
            out[:, start : start + LANES] = jnp.concatenate(parts[which], axis=1)


def attn_backward(kept, rows, grads, slots):
    images = kept.shape[0]
    width = rows.shape[1]
    return pl.pallas_call(
        attn_backward_body,
        out_shape=jax.ShapeDtypeStruct(rows.shape, BF16),
        grid_spec=pltpu.PrefetchScalarGridSpec(
            num_scalar_prefetch=1,
            grid=(images,),
            in_specs=[
                pl.BlockSpec((slots, width), lambda i, kept: (i, 0)),
                pl.BlockSpec((slots, width // 3), lambda i, kept: (i, 0)),
            ],
            out_specs=pl.BlockSpec((slots, width), lambda i, kept: (i, 0)),
        ),
        name="attn_backward",
    )(kept, rows, grads)


ERF_TOP = (
    -2.72614225801306e-10,
    2.77068142495902e-08,
    -2.10102402082508e-06,
    -5.69250639462346e-05,
    -7.34990630326855e-04,
    -2.95459980854025e-03,
    -1.60960333262415e-02,
)
ERF_BOTTOM = (
    -1.45660718464996e-05,
    -2.13374055278905e-04,
    -1.68282697438203e-03,
    -7.37332916720468e-03,
    -1.42647390514189e-02,
)


def erf(value):
    value = jnp.clip(value, -4.0, 4.0)
    square = value * value
    top = jnp.full_like(value, ERF_TOP[0])
    for factor in ERF_TOP[1:]:
        top = top * square + factor
    bottom = jnp.full_like(value, ERF_BOTTOM[0])
    for factor in ERF_BOTTOM[1:]:
        bottom = bottom * square + factor
    return value * top / bottom


def feed_body(rows, cot, up, down_t, bias, *refs):
    hidden, grad_pre, bias_sum = refs[-3:]
    pre = dot(rows[...], up[...], (1, 0)) + bias[...]
    grad_hidden = dot(cot[...], down_t[...], (1, 0))
    cdf = 0.5 + 0.5 * erf(pre * 0.7071067811865476)
    density = 0.3989422804014327 * jnp.exp(-0.5 * pre * pre)
    hidden[...] = (pre * cdf).astype(BF16)
    grad = (grad_hidden * (cdf + pre * density)).astype(BF16)
    grad_pre[...] = grad

    @pl.when(pl.program_id(1) == 0)
    def _():
        bias_sum[...] = jnp.zeros(bias_sum.shape, F32)

    bias_sum[...] += jnp.sum(grad.astype(F32), axis=0, keepdims=True)


def feed(rows, cot, up, down_t, bias, half, held, row_block, col_block):
    count, features = rows.shape
    width = up.shape[1]
    steps = count // row_block
    first = half * steps
    whole = jax.ShapeDtypeStruct((2 * count, width), BF16)
    big = pl.BlockSpec((row_block, col_block), lambda j, i: (first + i, j))
    passed = [pl.BlockSpec(memory_space=pl.ANY) for _ in held]
    return pl.pallas_call(
        feed_body,
        out_shape=(whole, whole, jax.ShapeDtypeStruct((1, width), F32)),
        grid=(width // col_block, steps),
        in_specs=[
            pl.BlockSpec((row_block, features), lambda j, i: (i, 0)),
            pl.BlockSpec((row_block, features), lambda j, i: (first + i, 0)),
            pl.BlockSpec((features, col_block), lambda j, i: (0, j)),
            pl.BlockSpec((features, col_block), lambda j, i: (0, j)),
            pl.BlockSpec((1, col_block), lambda j, i: (0, j)),
            *passed,
        ],
        out_specs=(big, big, pl.BlockSpec((1, col_block), lambda j, i: (0, j))),
        input_output_aliases={5: 0, 6: 1} if held else {},
        name="feed",
    )(rows, cot, up, down_t, bias, *held)


def slot_numbers(owner_list, capacity, owners):
    count = owner_list.shape[0]
    onehot = (owner_list[:, None] == jnp.arange(owners, dtype=jnp.int32)[None, :]).astype(BF16)
    order = jnp.arange(count, dtype=jnp.int32)
    before = (order[:, None] > order[None, :]).astype(BF16)
    earlier = dot(before, onehot, (1, 0))
    return owner_list * capacity + jnp.sum(earlier * onehot.astype(F32), axis=1).astype(jnp.int32)


def low_lanes():
    return lax.broadcasted_iota(jnp.int32, (BS // 2, LANES), 1) < BS


def to_parcel_body(indices_of, slots, *refs):
    *inputs, out = refs
    step = pl.program_id(0)

    @pl.when(step == 0)
    def _():
        out[...] = jnp.zeros(out.shape, out.dtype)

    low = low_lanes()
    for number, source in enumerate(inputs):
        rows, cols = source.shape
        for row in range(rows // BS):
            for pair in range(cols // LANES):
                window = pl.ds(pair * LANES, LANES)
                top = source[pl.ds(row * BS, BS // 2), window]
                bottom = source[pl.ds(row * BS + BS // 2, BS // 2), window]
                left, right = indices_of(number, step, row, pair)
                out[slots[left]] = jnp.where(low, top, pltpu.roll(bottom, BS, 1))
                out[slots[right]] = jnp.where(low, pltpu.roll(top, BS, 1), bottom)


def after(value, *others):
    return lax.optimization_barrier((value, *others))[0]


def to_parcel(slots, total, sources, indices_of):
    return pl.pallas_call(
        partial(to_parcel_body, indices_of),
        out_shape=jax.ShapeDtypeStruct((total, BS // 2, LANES), BF16),
        grid_spec=pltpu.PrefetchScalarGridSpec(
            num_scalar_prefetch=1,
            grid=(PARCEL_STEPS,),
            in_specs=[
                pl.BlockSpec((a.shape[0] // PARCEL_STEPS, a.shape[1]), lambda i, slots: (i, 0))
                for a in sources
            ],
            out_specs=pl.BlockSpec(
                (total, BS // 2, LANES), lambda i, slots: (0, 0, 0), pipeline_mode=pl.Buffered(1)
            ),
        ),
        name="to_parcel",
    )(slots, *sources)


PARCEL_STEPS = 4


def attn_parcel(slots, total, qkv_grad, out_grad):
    rows = qkv_grad.shape[0] // BS
    cols = out_grad.shape[0] // BS

    def indices_of(number, step, row, pair):
        if number == 0:
            matrix, col = divmod(2 * pair, cols)
            first = matrix * rows * cols + (step * (rows // PARCEL_STEPS) + row) * cols + col
        else:
            first = 3 * rows * cols + (step * (cols // PARCEL_STEPS) + row) * rows + 2 * pair
        return (first, first + 1)

    sources = (qkv_grad, out_grad)
    return to_parcel(slots, total, sources, indices_of)


def mlp_parcel(slots, total, up_grad, down_grad):
    rows = up_grad.shape[0] // BS
    cols = up_grad.shape[1] // BS

    def indices_of(number, step, row, pair):
        if number == 0:
            first = (step * (rows // PARCEL_STEPS) + row) * cols + 2 * pair
        else:
            first = rows * cols + (step * (cols // PARCEL_STEPS) + row) * rows + 2 * pair
        return (first, first + 1)

    return to_parcel(slots, total, (up_grad, down_grad), indices_of)


def pair_tile(left, right, low):
    top = jnp.where(low, left, pltpu.roll(right, BS, 1))
    bottom = jnp.where(low, pltpu.roll(left, BS, 1), right)
    return (top, bottom)


def local_blocks(place, rows, cols, own):
    matrix = jnp.arange(3, dtype=jnp.int32)[:, None, None]
    row = jnp.arange(own, dtype=jnp.int32)[None, :, None]
    col = jnp.arange(cols, dtype=jnp.int32)[None, None, :]
    first = ((matrix * rows + place * own + row) * cols + col).reshape(-1)
    row = jnp.arange(cols, dtype=jnp.int32)[:, None]
    col = jnp.arange(own, dtype=jnp.int32)[None, :]
    second = (3 * rows * cols + row * rows + place * own + col).reshape(-1)
    return jnp.concatenate([first, second])


def pick_body(table, held, *outs):
    count = outs[0].shape[0]
    for number, out in enumerate(outs):
        for block in range(count):
            out[block] = held[table[number * count + block]]


def pick(table, held, outs):
    whole = pl.BlockSpec(memory_space=pltpu.VMEM)
    shape = jax.ShapeDtypeStruct((table.shape[0] // outs,) + held.shape[1:], held.dtype)
    return pl.pallas_call(
        pick_body,
        out_shape=(shape,) * outs,
        in_specs=[pl.BlockSpec(memory_space=pltpu.SMEM), whole],
        out_specs=(whole,) * outs,
        name="pick",
    )(table, held)


def attn_finish_body(held, arrived, qkv_out, out_out):
    low = low_lanes()
    own = qkv_out.shape[1] // BS
    cols = qkv_out.shape[2] // BS

    def put(target, row, pair, first):
        top, bottom = pair_tile(held[first] + arrived[first], held[first + 1] + arrived[first + 1], low)
        window = pl.ds(pair * LANES, LANES)
        target[pl.ds(row * BS, BS // 2), window] = top
        target[pl.ds(row * BS + BS // 2, BS // 2), window] = bottom

    for matrix in range(3):
        for row in range(own):
            for pair in range(cols // 2):
                put(qkv_out.at[matrix], row, pair, (matrix * own + row) * cols + 2 * pair)
    for row in range(cols):
        for pair in range(own // 2):
            put(out_out, row, pair, 3 * own * cols + row * own + 2 * pair)


def attn_finish(held, arrived, shapes):
    whole = pl.BlockSpec(memory_space=pltpu.VMEM)
    return pl.pallas_call(
        attn_finish_body,
        out_shape=tuple(jax.ShapeDtypeStruct(shape, BF16) for shape in shapes),
        in_specs=[whole, whole],
        out_specs=tuple(whole for _ in shapes),
        name="attn_finish",
    )(held, arrived)


def mlp_return_body(rows, cols, slots, place, held, up_out, down_out):
    low = low_lanes()
    mine = place[0]
    own = up_out.shape[0] // BS

    def put(target, row, pair, first):
        top, bottom = pair_tile(held[slots[first]], held[slots[first + 1]], low)
        window = pl.ds(pair * LANES, LANES)
        target[pl.ds(row * BS, BS // 2), window] = top
        target[pl.ds(row * BS + BS // 2, BS // 2), window] = bottom

    for row in range(own):
        for pair in range(cols // 2):
            put(up_out, row, pair, (mine * own + row) * cols + 2 * pair)
    for row in range(cols):
        for pair in range(own // 2):
            put(down_out, row, pair, rows * cols + row * rows + mine * own + 2 * pair)


def from_slots(body, slots, place, held, shapes):
    whole = pl.BlockSpec(memory_space=pltpu.VMEM)
    table = pl.BlockSpec(memory_space=pltpu.SMEM)
    return pl.pallas_call(
        body,
        out_shape=tuple(jax.ShapeDtypeStruct(shape, BF16) for shape in shapes),
        in_specs=[table, table, whole],
        out_specs=tuple(whole for _ in shapes),
        name="from_slots",
    )(slots, place, held)


def unpack(dense):
    return jnp.concatenate([dense[:, :, :BS], dense[:, :, BS:]], axis=1)


def pack(blocks):
    return jnp.concatenate([blocks[:, : BS // 2], blocks[:, BS // 2 :]], axis=2)


def join_blocks(blocks_in, leading, row_count, col_count):
    shaped = blocks_in.reshape(leading + (row_count // BS, col_count // BS, BS, BS))
    depth = len(leading)
    axes_order = tuple(range(depth)) + (depth, depth + 2, depth + 1, depth + 3)
    return shaped.transpose(axes_order).reshape(leading + (row_count, col_count))


def soap_update(gradient, left_basis, right_basis, first_moment, second, master):
    turned = jnp.einsum("sji,sjk->sik", left_basis, gradient, precision=precise)
    turned = jnp.einsum("sik,skl->sil", turned, right_basis, precision=precise)
    first_new = 0.95 * first_moment + 0.05 * turned
    second_new = 0.95 * second + 0.05 * turned * turned
    direction = first_new / (jnp.sqrt(second_new) + 1e-08)
    rotated_back = jnp.einsum("sij,sjk->sik", left_basis, direction, precision=precise)
    rotated_back = jnp.einsum("sik,slk->sil", rotated_back, right_basis, precision=precise)
    return (first_new, second_new, master - 0.05 * rotated_back)


def per_device(
    tokens,
    kept_counts,
    cotangent,
    w_qkv,
    w_out,
    w_up,
    w_down,
    ln1_gain,
    ln1_bias,
    ln2_gain,
    ln2_bias,
    out_bias,
    up_bias,
    down_bias,
    attn_owner,
    mlp_owner,
    attn_left,
    attn_right,
    attn_first,
    attn_second,
    attn_master,
    mlp_left,
    mlp_right,
    mlp_first,
    mlp_second,
    mlp_master,
):
    head_pos = lax.axis_index("head")
    tensor_pos = lax.axis_index("tensor")
    shard_pos = lax.axis_index("shard")
    local_images, slot_count, features = tokens.shape
    per_out = local_images // 4
    own_rows = per_out * slot_count

    attn_mine = jnp.concatenate([w_qkv[0], w_qkv[1], w_qkv[2], w_out.T], axis=1)
    attn_full = lax.all_gather(attn_mine, "shard", axis=0, tiled=True)
    group_cols = w_qkv.shape[2]
    qkv_full = attn_full[:, : 3 * group_cols]
    out_full_t = attn_full[:, 3 * group_cols :]
    mlp_mine = lax.all_gather(
        jnp.where(head_pos == 0, w_up, w_down.T), "shard", axis=0, tiled=True
    )
    hidden_cols = mlp_mine.shape[1]

    def images_of(array, start):
        return lax.dynamic_slice_in_dim(array, start * per_out, per_out, 0)

    own_index = head_pos * 2 + tensor_pos
    pair_index = (1 - head_pos) * 2 + tensor_pos
    attn_tokens = jnp.concatenate([images_of(tokens, own_index), images_of(tokens, pair_index)])
    attn_tokens = attn_tokens.reshape(2 * own_rows, features)
    own_kept = images_of(kept_counts, own_index)
    attn_kept = jnp.concatenate([own_kept, images_of(kept_counts, pair_index)])
    mlp_kept = jnp.concatenate([own_kept, images_of(kept_counts, head_pos * 2 + 1 - tensor_pos)])
    mlp_cot = jnp.concatenate([images_of(cotangent, tensor_pos), images_of(cotangent, 1 - tensor_pos)])
    positions = jnp.arange(slot_count, dtype=jnp.int32)
    mlp_valid = positions[None, :] < (BUF + mlp_kept)[:, None]
    mlp_cot = jnp.where(mlp_valid[:, :, None], mlp_cot, jnp.zeros_like(mlp_cot))
    mlp_cot = mlp_cot.reshape(2 * own_rows, features)
    own_valid = mlp_valid[:per_out].reshape(own_rows, 1).astype(F32)
    own_cot = mlp_cot[:own_rows].astype(F32)

    normed_one, inv_one = norm_parts(attn_tokens.astype(F32))
    low_one = (normed_one * ln1_gain + ln1_bias).astype(BF16)
    projected = dot(low_one, qkv_full, (1, 0)).astype(BF16)
    heads_out = attn_forward(attn_kept, projected, slot_count)
    pair_branch = dot(heads_out[own_rows:], out_full_t, (1, 1)).astype(BF16)
    branch_in = swap(pair_branch, "head")
    own_branch = dot(heads_out[:own_rows], out_full_t, (1, 1))
    residual = attn_tokens[:own_rows].astype(F32) + (own_branch + branch_in.astype(F32)) + out_bias
    normed_two, inv_two = norm_parts(residual)
    low_two = (normed_two * ln2_gain + ln2_bias).astype(BF16)

    low_in = swap(low_two, "tensor")
    mlp_mine = after(mlp_mine, low_in)
    mlp_other = swap(mlp_mine, "head")
    up_full = jnp.where(head_pos == 0, mlp_mine, mlp_other)
    down_full_t = jnp.where(head_pos == 0, mlp_other, mlp_mine)
    up_local = lax.dynamic_slice_in_dim(up_bias, tensor_pos * hidden_cols, hidden_cols, 0)[None]
    hidden_half, pre_half, pair_sum = feed(
        low_in, mlp_cot, up_full, down_full_t, up_local, 1, (), slot_count, 512
    )
    pair_normed = dot(pre_half[own_rows:], up_full, (1, 1)).astype(BF16)
    normed_in = swap(pair_normed, "tensor")
    hidden, grad_pre, own_sum = feed(
        low_two, mlp_cot, up_full, down_full_t, up_local, 0,
        (hidden_half, after(pre_half, pair_normed)), slot_count, 512,
    )
    up_bias_part = pair_sum + own_sum
    own_grad_normed = dot(grad_pre[:own_rows], up_full, (1, 1))
    normed_rows = jnp.concatenate([low_two, low_in])
    up_grad = dot(normed_rows, grad_pre, (0, 0)).astype(BF16)
    down_grad = dot(hidden, mlp_cot, (0, 0)).astype(BF16)
    mlp_owners = lax.axis_size(("shard", "head"))
    mlp_cap = mlp_master.shape[1]
    mlp_slots = slot_numbers(mlp_owner[0, :, 0], mlp_cap, mlp_owners)
    mlp_parts = mlp_parcel(mlp_slots, mlp_owners * mlp_cap, up_grad, down_grad)
    mlp_sum = lax.psum_scatter(mlp_parts, ("shard", "head"), scatter_dimension=0, tiled=True)
    pair_mlp = dot(hidden[own_rows:], down_full_t, (1, 1)).astype(BF16)
    mlp_in = swap(pair_mlp, "tensor")
    own_mlp = dot(hidden[:own_rows], down_full_t, (1, 1))
    mlp_out = own_mlp + mlp_in.astype(F32) + down_bias
    out = (own_valid * (residual + mlp_out)).astype(BF16)
    resid_from, ln2_gain_part, ln2_bias_part = norm_back(
        own_grad_normed + normed_in.astype(F32), normed_two, inv_two, ln2_gain
    )
    down_bias_part = jnp.sum(own_cot, axis=0)
    grad_resid = own_cot + resid_from
    grad_branch = grad_resid.astype(BF16)
    out_bias_part = jnp.sum(grad_branch.astype(F32), axis=0)

    branch_rows = jnp.concatenate([grad_branch, after(swap(grad_branch, "head"), mlp_parts)])
    grad_heads = dot(branch_rows, out_full_t, (1, 0)).astype(BF16)
    grad_proj = attn_backward(attn_kept, projected, grad_heads, slot_count)
    out_grad = dot(heads_out, branch_rows, (0, 0)).astype(BF16)
    qkv_grad = dot(low_one, grad_proj, (0, 0)).astype(BF16)
    pair_input = dot(grad_proj[own_rows:], qkv_full, (1, 1)).astype(BF16)
    input_in = swap(pair_input, "head")
    own_input = dot(grad_proj[:own_rows], qkv_full, (1, 1))
    tokens_from, ln1_gain_part, ln1_bias_part = norm_back(
        own_input + input_in.astype(F32), normed_one[:own_rows], inv_one[:own_rows], ln1_gain
    )
    tokens_grad = grad_resid + tokens_from

    up_whole = lax.dynamic_update_slice_in_dim(
        jnp.zeros((FF,), F32), up_bias_part[0], tensor_pos * hidden_cols, 0
    )
    small = jnp.concatenate(
        [
            ln1_gain_part,
            ln1_bias_part,
            ln2_gain_part,
            ln2_bias_part,
            out_bias_part,
            down_bias_part,
            up_whole,
        ]
    ).reshape(-1, LANES)
    small = total_over_mesh(small).reshape(-1)
    small_sums = [small[i * features : (i + 1) * features] for i in range(6)] + [small[6 * features :]]

    place = shard_pos.reshape(1).astype(jnp.int32)
    rows = features // BS

    shards = lax.axis_size("shard")
    tensors = lax.axis_size("tensor")
    attn_owners = shards * tensors
    attn_cap = attn_master.shape[1]
    attn_total = attn_owners * attn_cap
    attn_slots = slot_numbers(attn_owner[0, :, 0], attn_cap, attn_owners)
    direct = shards == 8 and tensors == 2
    if direct:
        owner = attn_owner[0, :, 0]
        inner = attn_slots - owner * attn_cap
        off_tensor = (owner % tensors) ^ tensor_pos
        off_shard = (owner // tensors) ^ shard_pos
        bit, high = off_shard % 2, off_shard // 2
        columns = shards // 2
        sizes = ((attn_cap + 1) // 2, attn_cap // 2)
        start = attn_owners * sizes[0]
        spot = jnp.where(
            inner < sizes[0],
            ((off_tensor * 2 + bit) * columns + high) * sizes[0] + inner,
            start + ((bit * 2 + off_tensor) * columns + high) * sizes[1] + inner - sizes[0],
        )
        parts = attn_parcel(spot, attn_total, qkv_grad, out_grad)

        def across(value, bits):
            return lax.ppermute(value, "shard", [(i, i ^ bits) for i in range(shards)])

        def so_far(which, first, count, arrived):
            size = columns * sizes[which]
            begin = which * start
            total = parts[begin + first * size : begin + first * size + count].astype(F32)
            for array in arrived:
                total = total + array[first * size : first * size + count].astype(F32)
            return total

        spans = [columns * size for size in sizes]
        first_a = swap(parts[2 * spans[0] : 4 * spans[0]], "tensor")
        first_b = across(parts[start + 2 * spans[1] : start + 4 * spans[1]], 1)
        next_a = so_far(0, 1, spans[0], (first_a,)).astype(BF16)
        next_b = so_far(1, 1, spans[1], (first_b,)).astype(BF16)
        mlp_sum = after(mlp_sum, next_a, next_b)
        second_a = across(next_a, 1)
        second_b = swap(next_b, "tensor")
        sums = jnp.concatenate(
            [
                so_far(0, 0, spans[0], (first_a, second_a)).reshape(columns, sizes[0], BS // 2, LANES),
                so_far(1, 0, spans[1], (first_b, second_b)).reshape(columns, sizes[1], BS // 2, LANES),
            ],
            axis=1,
        )
        attn_sum = sums[0]
        for step in range(1, columns):
            attn_sum = attn_sum + across(sums[step].astype(BF16), 2 * step).astype(F32)
    else:
        parts = attn_parcel(attn_slots, attn_total, qkv_grad, out_grad)
        attn_sum = lax.psum_scatter(parts, ("shard", "tensor"), scatter_dimension=0, tiled=True)
    attn_sum = unpack(attn_sum).astype(F32)
    mlp_sum = unpack(mlp_sum).astype(F32)

    mlp_first_new, mlp_second_new, mlp_master_new = soap_update(
        mlp_sum, mlp_left[0], mlp_right[0], mlp_first[0], mlp_second[0], mlp_master[0]
    )
    mlp_dense = pack(mlp_master_new.astype(BF16))
    if direct:
        mlp_dense = after(mlp_dense, second_a, second_b)
    mlp_all = lax.all_gather(mlp_dense, ("shard", "head"), axis=0, tiled=True)
    mlp_outs = lax.optimization_barrier(
        tuple(jnp.transpose(a, (1, 2, 0)) for a in (mlp_sum, mlp_first_new, mlp_second_new, mlp_master_new))
    )
    attn_first_new, attn_second_new, attn_master_new = soap_update(
        attn_sum, attn_left[0], attn_right[0], attn_first[0], attn_second[0], attn_master[0]
    )
    attn_dense = pack(attn_master_new.astype(BF16))

    own = w_qkv.shape[1]
    if direct:
        column = [attn_dense] + [across(attn_dense, 2 * step) for step in range(1, columns)]
        empty = jnp.zeros((1,) + attn_dense.shape[1:], BF16)
        here = (off_tensor == 0) & (bit == 0)
        where = jnp.where(here, high * attn_cap + inner, columns * attn_cap)
        lists = [local_blocks(p, rows, group_cols // BS, own // BS) for p in (shard_pos, shard_pos ^ 1)]
        table = jnp.take(where, jnp.concatenate(lists), axis=0)
        mine, theirs = pick(after(table, *mlp_outs), jnp.concatenate(column + [empty]), 2)
        mine = mine + across(theirs, 1)
        w_qkv_new, w_out_new = attn_finish(mine, swap(mine, "tensor"), (w_qkv.shape, w_out.shape))
        w_up_new, w_down_new = from_slots(
            partial(mlp_return_body, rows, hidden_cols // BS),
            mlp_slots,
            place,
            mlp_all,
            (w_up.shape, w_down.shape),
        )
    else:
        attn_all = lax.all_gather(attn_dense, ("shard", "tensor"), axis=0, tiled=True)
        attn_new = unpack(jnp.take(attn_all, attn_slots, axis=0))
        qkv_count = 3 * rows * (group_cols // BS)
        new_qkv = join_blocks(attn_new[:qkv_count], (3,), features, group_cols)
        new_out = join_blocks(attn_new[qkv_count:], (), group_cols, features)
        w_qkv_new = lax.dynamic_slice_in_dim(new_qkv, shard_pos * own, own, 1)
        w_out_new = lax.dynamic_slice_in_dim(new_out, shard_pos * own, own, 1)
        mlp_new = unpack(jnp.take(mlp_all, mlp_slots, axis=0))
        up_count = rows * (hidden_cols // BS)
        new_up = join_blocks(mlp_new[:up_count], (), features, hidden_cols)
        new_down = join_blocks(mlp_new[up_count:], (), hidden_cols, features)
        w_up_new = lax.dynamic_slice_in_dim(new_up, shard_pos * own, own, 0)
        w_down_new = lax.dynamic_slice_in_dim(new_down, shard_pos * own, own, 1)

    return (
        out.reshape(per_out, slot_count, features),
        tokens_grad.reshape(per_out, slot_count, features),
        *small_sums,
        attn_sum[None],
        attn_first_new[None],
        attn_second_new[None],
        attn_master_new[None],
        *(jnp.transpose(array, (2, 0, 1))[None] for array in mlp_outs),
        w_qkv_new,
        w_out_new,
        w_up_new,
        w_down_new,
    )


def solution(mesh):
    placed = (
        P("shard", None, None),
        P("shard"),
        P(("shard", "head"), None, None),
        P(None, "shard", "head"),
        P("head", "shard"),
        P("shard", "tensor"),
        P("tensor", "shard"),
        P(),
        P(),
        P(),
        P(),
        P(),
        P(),
        P(),
        P("head", None, None),
        P("tensor", None, None),
        P("head", ("shard", "tensor"), None, None),
        P("head", ("shard", "tensor"), None, None),
        P("head", ("shard", "tensor"), None, None),
        P("head", ("shard", "tensor"), None, None),
        P("head", ("shard", "tensor"), None, None),
        P("tensor", ("shard", "head"), None, None),
        P("tensor", ("shard", "head"), None, None),
        P("tensor", ("shard", "head"), None, None),
        P("tensor", ("shard", "head"), None, None),
        P("tensor", ("shard", "head"), None, None),
    )
    return jax.shard_map(
        per_device,
        mesh=mesh,
        in_specs=placed,
        out_specs=(
            P(("shard", "head", "tensor"), None, None),
            P(("shard", "head", "tensor"), None, None),
            P(),
            P(),
            P(),
            P(),
            P(),
            P(),
            P(),
            P("head", ("shard", "tensor"), None, None),
            P("head", ("shard", "tensor"), None, None),
            P("head", ("shard", "tensor"), None, None),
            P("head", ("shard", "tensor"), None, None),
            P("tensor", ("shard", "head"), None, None),
            P("tensor", ("shard", "head"), None, None),
            P("tensor", ("shard", "head"), None, None),
            P("tensor", ("shard", "head"), None, None),
            P(None, "shard", "head"),
            P("head", "shard"),
            P("shard", "tensor"),
            P("tensor", "shard"),
        ),
        check_vma=False,
    )
```

```python
from functools import partial

import jax
import jax.numpy as jnp
from jax import lax
from jax.experimental import pallas as pl
from jax.experimental.pallas import tpu as pltpu
from jax.sharding import PartitionSpec as P


HD = 64
FF = 4096
BUF = 64
BS = 64
LANES = 128
SHARD, HEAD, TENSOR = "shard", "head", "tensor"
F32 = jnp.float32
BF16 = jnp.bfloat16

precise = lax.Precision.HIGHEST


def swap(value, axis):
    return lax.ppermute(value, axis, [(0, 1), (1, 0)])


def across(value, bits):
    size = lax.axis_size(SHARD)
    return lax.ppermute(value, SHARD, [(i, i ^ bits) for i in range(size)])


def settle(*arrays):
    anywhere = pl.BlockSpec(memory_space=pl.ANY)
    return pl.pallas_call(
        lambda *refs: None,
        out_shape=tuple(jax.ShapeDtypeStruct(a.shape, a.dtype) for a in arrays),
        in_specs=[anywhere] * len(arrays),
        out_specs=(anywhere,) * len(arrays),
        input_output_aliases={i: i for i in range(len(arrays))},
        name="settle",
    )(*arrays)


def dot(left, right, contract):
    return lax.dot_general(left, right, ((contract[:1], contract[1:]), ((), ())), preferred_element_type=F32)


def norm_parts(value):
    center = value - jnp.mean(value, axis=-1, keepdims=True)
    inv_root = lax.rsqrt(jnp.mean(center * center, axis=-1, keepdims=True) + 1e-06)
    return (center * inv_root, inv_root)


def norm_back(grad_out, normed, inv_root, gain_vec):
    grad_normed = grad_out * gain_vec
    first_mean = jnp.mean(grad_normed, axis=-1, keepdims=True)
    second_mean = jnp.mean(grad_normed * normed, axis=-1, keepdims=True)
    grad_in = inv_root * (grad_normed - first_mean - normed * second_mean)
    return (grad_in, jnp.sum(grad_out * normed, axis=0), jnp.sum(grad_out, axis=0))


def head_pair(rows, pair, which):
    groups = rows.shape[1] // (3 * HD)
    first = which * groups * HD + pair * LANES
    return rows[:, first : first + LANES]


def one_head_each(both):
    first = lax.broadcasted_iota(jnp.int32, both.shape, 0) < HD
    nothing = jnp.zeros_like(both)
    return (jnp.where(first, both, nothing), jnp.where(first, nothing, both))


def weights_of(keys, queries, valid):
    scores = jnp.where(valid, dot(keys, queries, (1, 0)), -1000000000.0)
    raised = jnp.exp(scores - jnp.max(scores, axis=0, keepdims=True))
    return (raised, 1.0 / jnp.sum(raised, axis=0, keepdims=True))


def key_mask(rows, count):
    slots = rows.shape[0]
    return lax.broadcasted_iota(jnp.int32, (slots, slots), 0) < BUF + count


def attn_forward_body(kept, rows, out):
    valid = key_mask(rows, kept[pl.program_id(0)])
    for pair in range(rows.shape[1] // (6 * HD)):
        queries = (head_pair(rows, pair, 0) * jnp.asarray(0.125, BF16)).T
        keys = head_pair(rows, pair, 1)
        values = head_pair(rows, pair, 2).T
        halves = []
        for number, query in enumerate(one_head_each(queries)):
            raised, scale = weights_of(keys, query, valid)
            value = values[number * HD : (number + 1) * HD]
            halves.append(dot(value, raised.astype(BF16), (1, 0)) * scale)
        out[:, pair * LANES : (pair + 1) * LANES] = jnp.concatenate(halves).T.astype(BF16)


def attn_forward(kept, rows, slots):
    images = kept.shape[0]
    width = rows.shape[1]
    return pl.pallas_call(
        attn_forward_body,
        out_shape=jax.ShapeDtypeStruct((images * slots, width // 3), BF16),
        grid_spec=pltpu.PrefetchScalarGridSpec(
            num_scalar_prefetch=1,
            grid=(images,),
            in_specs=[pl.BlockSpec((slots, width), lambda i, kept: (i, 0))],
            out_specs=pl.BlockSpec((slots, width // 3), lambda i, kept: (i, 0)),
        ),
        name="attn_forward",
    )(kept, rows)


def attn_backward_body(kept, rows, grads, out):
    valid = key_mask(rows, kept[pl.program_id(0)])
    width = rows.shape[1] // 3
    first = lax.broadcasted_iota(jnp.int32, (rows.shape[0], LANES), 1) < HD
    for pair in range(width // LANES):
        window = slice(pair * LANES, (pair + 1) * LANES)
        queries = head_pair(rows, pair, 0) * jnp.asarray(0.125, BF16)
        keys = head_pair(rows, pair, 1)
        keys_t = keys.T
        values = head_pair(rows, pair, 2)
        grad = grads[:, window]
        halves = ([], [], [])
        for number, (query, grad_t) in enumerate(zip(one_head_each(queries.T), one_head_each(grad.T))):
            raised, scale = weights_of(keys, query, valid)
            probs = raised * scale
            grad_probs = dot(values, grad_t, (1, 0))
            inner = jnp.sum(probs * grad_probs, axis=0, keepdims=True)
            grad_scores = (probs * (grad_probs - inner)).astype(BF16)
            halves[0].append(dot(keys_t[number * HD : (number + 1) * HD], grad_scores, (1, 0)))
            halves[1].append(dot(grad_scores, queries, (1, 0)))
            halves[2].append(dot(probs.astype(BF16), grad, (1, 0)))
        out[:, window] = (jnp.concatenate(halves[0]).T * 0.125).astype(BF16)
        for which in (1, 2):
            start = which * width + pair * LANES
            out[:, start : start + LANES] = jnp.where(first, *halves[which]).astype(BF16)


def attn_backward(kept, rows, grads, slots):
    images = kept.shape[0]
    width = rows.shape[1]
    return pl.pallas_call(
        attn_backward_body,
        out_shape=jax.ShapeDtypeStruct(rows.shape, BF16),
        grid_spec=pltpu.PrefetchScalarGridSpec(
            num_scalar_prefetch=1,
            grid=(images,),
            in_specs=[
                pl.BlockSpec((slots, width), lambda i, kept: (i, 0)),
                pl.BlockSpec((slots, width // 3), lambda i, kept: (i, 0)),
            ],
            out_specs=pl.BlockSpec((slots, width), lambda i, kept: (i, 0)),
        ),
        name="attn_backward",
    )(kept, rows, grads)


ERF_TOP = (
    -2.72614225801306e-10,
    2.77068142495902e-08,
    -2.10102402082508e-06,
    -5.69250639462346e-05,
    -7.34990630326855e-04,
    -2.95459980854025e-03,
    -1.60960333262415e-02,
)
ERF_BOTTOM = (
    -1.45660718464996e-05,
    -2.13374055278905e-04,
    -1.68282697438203e-03,
    -7.37332916720468e-03,
    -1.42647390514189e-02,
)


def erf(value):
    value = jnp.clip(value, -4.0, 4.0)
    square = value * value
    top = jnp.full_like(value, ERF_TOP[0])
    for factor in ERF_TOP[1:]:
        top = top * square + factor
    bottom = jnp.full_like(value, ERF_BOTTOM[0])
    for factor in ERF_BOTTOM[1:]:
        bottom = bottom * square + factor
    return value * top / bottom


COL_CHUNK = 256


def feed_body(flag, rows, cot, mine, other, bias, *refs):
    hidden, grad_pre, bias_sum, grad_rows, up, down_t, total = refs[-7:]
    step = pl.program_id(0)
    for swapped in (False, True):

        @pl.when((flag[0] != 0) == swapped)
        def _():
            up[...] = other[...] if swapped else mine[...]
            down_t[...] = mine[...] if swapped else other[...]

    part = None
    for start in range(0, up.shape[1], COL_CHUNK):
        window = slice(start, start + COL_CHUNK)
        pre = dot(rows[...], up[:, window], (1, 0)) + bias[:, window]
        grad_hidden = dot(cot[...], down_t[:, window], (1, 0))
        cdf = 0.5 + 0.5 * erf(pre * 0.7071067811865476)
        density = 0.3989422804014327 * jnp.exp(-0.5 * pre * pre)
        hidden[:, window] = (pre * cdf).astype(BF16)
        grad = (grad_hidden * (cdf + pre * density)).astype(BF16)
        grad_pre[:, window] = grad
        bias_sum[:, window] = jnp.sum(grad.astype(F32), axis=0, keepdims=True)
        back = dot(grad, up[:, window], (1, 1))
        part = back if part is None else part + back

    @pl.when(step == 0)
    def _():
        total[...] = part

    @pl.when(step > 0)
    def _():
        total[...] += part

    @pl.when(step == pl.num_programs(0) - 1)
    def _():
        grad_rows[...] = total[...].astype(grad_rows.dtype)


def feed(flag, rows, cot, mine, other, bias, half, held, col_block, grad_type):
    count, features = rows.shape
    width = mine.shape[1]
    whole = jax.ShapeDtypeStruct((2 * count, width), BF16)
    big = pl.BlockSpec((count, col_block), lambda j: (half, j))
    weight = pl.BlockSpec((features, col_block), lambda j: (0, j))
    line = pl.BlockSpec((1, col_block), lambda j: (0, j))
    passed = [pl.BlockSpec(memory_space=pl.ANY) for _ in held]
    return pl.pallas_call(
        feed_body,
        out_shape=(
            whole,
            whole,
            jax.ShapeDtypeStruct((1, width), F32),
            jax.ShapeDtypeStruct((count, features), grad_type),
        ),
        grid=(width // col_block,),
        in_specs=[
            pl.BlockSpec(memory_space=pltpu.SMEM),
            pl.BlockSpec((count, features), lambda j: (0, 0)),
            pl.BlockSpec((count, features), lambda j: (half, 0)),
            weight,
            weight,
            line,
            *passed,
        ],
        out_specs=(big, big, line, pl.BlockSpec((count, features), lambda j: (0, 0))),
        scratch_shapes=[
            pltpu.VMEM((features, col_block), BF16),
            pltpu.VMEM((features, col_block), BF16),
            pltpu.VMEM((count, features), F32),
        ],
        input_output_aliases={6: 0, 7: 1} if held else {},
        name="feed",
    )(flag, rows, cot, mine, other, bias, *held)


def slot_numbers(owner_list, capacity, owners):
    count = owner_list.shape[0]
    onehot = (owner_list[:, None] == jnp.arange(owners, dtype=jnp.int32)[None, :]).astype(BF16)
    order = jnp.arange(count, dtype=jnp.int32)
    before = (order[:, None] > order[None, :]).astype(BF16)
    earlier = dot(before, onehot, (1, 0))
    return owner_list * capacity + jnp.sum(earlier * onehot.astype(F32), axis=1).astype(jnp.int32)


def low_lanes():
    return lax.broadcasted_iota(jnp.int32, (BS // 2, LANES), 1) < BS


def to_parcel_body(indices_of, slots, *refs):
    *inputs, out = refs
    step = pl.program_id(0)

    @pl.when(step == 0)
    def _():
        out[...] = jnp.zeros(out.shape, out.dtype)

    low = low_lanes()
    for number, source in enumerate(inputs):
        rows, cols = source.shape
        for row in range(rows // BS):
            for pair in range(cols // LANES):
                window = pl.ds(pair * LANES, LANES)
                top = source[pl.ds(row * BS, BS // 2), window]
                bottom = source[pl.ds(row * BS + BS // 2, BS // 2), window]
                left, right = indices_of(number, step, row, pair)
                out[slots[left]] = jnp.where(low, top, pltpu.roll(bottom, BS, 1))
                out[slots[right]] = jnp.where(low, pltpu.roll(top, BS, 1), bottom)


def after(value, *others):
    return lax.optimization_barrier((value, *others))[0]


def to_parcel(slots, total, sources, indices_of):
    return pl.pallas_call(
        partial(to_parcel_body, indices_of),
        out_shape=jax.ShapeDtypeStruct((total, BS // 2, LANES), BF16),
        grid_spec=pltpu.PrefetchScalarGridSpec(
            num_scalar_prefetch=1,
            grid=(PARCEL_STEPS,),
            in_specs=[
                pl.BlockSpec((a.shape[0] // PARCEL_STEPS, a.shape[1]), lambda i, slots: (i, 0))
                for a in sources
            ],
            out_specs=pl.BlockSpec(
                (total, BS // 2, LANES), lambda i, slots: (0, 0, 0), pipeline_mode=pl.Buffered(1)
            ),
        ),
        name="to_parcel",
    )(slots, *sources)


PARCEL_STEPS = 4


def attn_parcel(slots, total, qkv_grad, out_grad):
    rows = qkv_grad.shape[0] // BS
    cols = out_grad.shape[0] // BS

    def indices_of(number, step, row, pair):
        if number == 0:
            matrix, col = divmod(2 * pair, cols)
            first = matrix * rows * cols + (step * (rows // PARCEL_STEPS) + row) * cols + col
        else:
            first = 3 * rows * cols + (step * (cols // PARCEL_STEPS) + row) * rows + 2 * pair
        return (first, first + 1)

    sources = (qkv_grad, out_grad)
    return to_parcel(slots, total, sources, indices_of)


def mlp_parcel(slots, total, up_grad, down_grad):
    rows = up_grad.shape[0] // BS
    cols = up_grad.shape[1] // BS

    def indices_of(number, step, row, pair):
        if number == 0:
            first = (step * (rows // PARCEL_STEPS) + row) * cols + 2 * pair
        else:
            first = rows * cols + (step * (cols // PARCEL_STEPS) + row) * rows + 2 * pair
        return (first, first + 1)

    return to_parcel(slots, total, (up_grad, down_grad), indices_of)


def pair_tile(left, right, low):
    top = jnp.where(low, left, pltpu.roll(right, BS, 1))
    bottom = jnp.where(low, pltpu.roll(left, BS, 1), right)
    return (top, bottom)


def local_blocks(place, rows, cols, own):
    matrix = jnp.arange(3, dtype=jnp.int32)[:, None, None]
    row = jnp.arange(own, dtype=jnp.int32)[None, :, None]
    col = jnp.arange(cols, dtype=jnp.int32)[None, None, :]
    first = ((matrix * rows + place * own + row) * cols + col).reshape(-1)
    row = jnp.arange(cols, dtype=jnp.int32)[:, None]
    col = jnp.arange(own, dtype=jnp.int32)[None, :]
    second = (3 * rows * cols + row * rows + place * own + col).reshape(-1)
    return jnp.concatenate([first, second])


def pick_body(table, held, *outs):
    count = outs[0].shape[0]
    for number, out in enumerate(outs):
        for block in range(count):
            out[block] = held[table[number * count + block]]


def pick(table, held, outs):
    whole = pl.BlockSpec(memory_space=pltpu.VMEM)
    shape = jax.ShapeDtypeStruct((table.shape[0] // outs,) + held.shape[1:], held.dtype)
    return pl.pallas_call(
        pick_body,
        out_shape=(shape,) * outs,
        in_specs=[pl.BlockSpec(memory_space=pltpu.SMEM), whole],
        out_specs=(whole,) * outs,
        name="pick",
    )(table, held)


def attn_finish_body(held, arrived, qkv_out, out_out):
    low = low_lanes()
    own = qkv_out.shape[1] // BS
    cols = qkv_out.shape[2] // BS

    def put(target, row, pair, first):
        top, bottom = pair_tile(held[first] + arrived[first], held[first + 1] + arrived[first + 1], low)
        window = pl.ds(pair * LANES, LANES)
        target[pl.ds(row * BS, BS // 2), window] = top
        target[pl.ds(row * BS + BS // 2, BS // 2), window] = bottom

    for matrix in range(3):
        for row in range(own):
            for pair in range(cols // 2):
                put(qkv_out.at[matrix], row, pair, (matrix * own + row) * cols + 2 * pair)
    for row in range(cols):
        for pair in range(own // 2):
            put(out_out, row, pair, 3 * own * cols + row * own + 2 * pair)


def attn_finish(held, arrived, shapes):
    whole = pl.BlockSpec(memory_space=pltpu.VMEM)
    return pl.pallas_call(
        attn_finish_body,
        out_shape=tuple(jax.ShapeDtypeStruct(shape, BF16) for shape in shapes),
        in_specs=[whole, whole],
        out_specs=tuple(whole for _ in shapes),
        name="attn_finish",
    )(held, arrived)


def mlp_return_body(rows, cols, slots, place, held, up_out, down_out):
    low = low_lanes()
    mine = place[0]
    own = up_out.shape[0] // BS

    def put(target, row, pair, first):
        top, bottom = pair_tile(held[slots[first]], held[slots[first + 1]], low)
        window = pl.ds(pair * LANES, LANES)
        target[pl.ds(row * BS, BS // 2), window] = top
        target[pl.ds(row * BS + BS // 2, BS // 2), window] = bottom

    for row in range(own):
        for pair in range(cols // 2):
            put(up_out, row, pair, (mine * own + row) * cols + 2 * pair)
    for row in range(cols):
        for pair in range(own // 2):
            put(down_out, row, pair, rows * cols + row * rows + mine * own + 2 * pair)


def from_slots(body, slots, place, held, shapes):
    whole = pl.BlockSpec(memory_space=pltpu.VMEM)
    table = pl.BlockSpec(memory_space=pltpu.SMEM)
    return pl.pallas_call(
        body,
        out_shape=tuple(jax.ShapeDtypeStruct(shape, BF16) for shape in shapes),
        in_specs=[table, table, whole],
        out_specs=tuple(whole for _ in shapes),
        name="from_slots",
    )(slots, place, held)


def add_up_body(*refs):
    *inputs, out = refs
    total = inputs[0][...].astype(F32)
    for source in inputs[1:]:
        total += source[...].astype(F32)
    out[:, : BS // 2, :] = total[:, :, :BS]
    out[:, BS // 2 :, :] = total[:, :, BS:]


def add_up(first, others):
    whole = pl.BlockSpec(memory_space=pltpu.VMEM)
    return pl.pallas_call(
        add_up_body,
        out_shape=jax.ShapeDtypeStruct((first.shape[0], BS, BS), F32),
        in_specs=[whole] * (1 + len(others)),
        out_specs=whole,
        name="add_up",
    )(first, *others)


def unpack(dense):
    return jnp.concatenate([dense[:, :, :BS], dense[:, :, BS:]], axis=1)


def pack(blocks):
    return jnp.concatenate([blocks[:, : BS // 2], blocks[:, BS // 2 :]], axis=2)


def join_blocks(blocks_in, leading, row_count, col_count):
    shaped = blocks_in.reshape(leading + (row_count // BS, col_count // BS, BS, BS))
    depth = len(leading)
    axes_order = tuple(range(depth)) + (depth, depth + 2, depth + 1, depth + 3)
    return shaped.transpose(axes_order).reshape(leading + (row_count, col_count))


def soap_update(gradient, left_basis, right_basis, first_moment, second, master):
    turned = jnp.einsum("sji,sjk->sik", left_basis, gradient, precision=precise)
    turned = jnp.einsum("sik,skl->sil", turned, right_basis, precision=precise)
    first_new = 0.95 * first_moment + 0.05 * turned
    second_new = 0.95 * second + 0.05 * turned * turned
    direction = first_new / (jnp.sqrt(second_new) + 1e-08)
    rotated_back = jnp.einsum("sij,sjk->sik", left_basis, direction, precision=precise)
    rotated_back = jnp.einsum("sik,slk->sil", rotated_back, right_basis, precision=precise)
    return (first_new, second_new, master - 0.05 * rotated_back)


def per_device(
    tokens,
    kept_counts,
    cotangent,
    w_qkv,
    w_out,
    w_up,
    w_down,
    ln1_gain,
    ln1_bias,
    ln2_gain,
    ln2_bias,
    out_bias,
    up_bias,
    down_bias,
    attn_owner,
    mlp_owner,
    attn_left,
    attn_right,
    attn_first,
    attn_second,
    attn_master,
    mlp_left,
    mlp_right,
    mlp_first,
    mlp_second,
    mlp_master,
):
    head_pos = lax.axis_index(HEAD)
    tensor_pos = lax.axis_index(TENSOR)
    shard_pos = lax.axis_index(SHARD)
    local_images, slot_count, features = tokens.shape
    per_out = local_images // 4
    own_rows = per_out * slot_count

    group_cols = w_qkv.shape[2]
    attn_mine = jnp.concatenate([w_qkv[0], w_qkv[1], w_qkv[2], w_out.T], axis=1)
    if lax.axis_size(TENSOR) == 2 and attn_mine.shape[0] % 32 == 0:
        half_rows = attn_mine.shape[0] // 2
        attn_half = lax.dynamic_slice_in_dim(attn_mine, tensor_pos * half_rows, half_rows, 0)
        attn_half = lax.all_gather(attn_half, SHARD, axis=0)
        first = tensor_pos == 0

        def both_halves(held):
            other = swap(held, TENSOR)
            parts = [jnp.where(first, held, other), jnp.where(first, other, held)]
            return jnp.stack(parts, axis=1).reshape(features, held.shape[2])

        qkv_full = both_halves(attn_half[:, :, : 3 * group_cols])
        out_full_t = both_halves(after(attn_half[:, :, 3 * group_cols :], qkv_full))
    else:
        attn_full = lax.all_gather(attn_mine, SHARD, axis=0, tiled=True)
        qkv_full = attn_full[:, : 3 * group_cols]
        out_full_t = attn_full[:, 3 * group_cols :]
    mlp_mine = lax.all_gather(
        after(jnp.where(head_pos == 0, w_up, w_down.T), attn_mine), SHARD, axis=0, tiled=True
    )
    hidden_cols = mlp_mine.shape[1]
    mlp_state = settle(mlp_left[0], mlp_right[0], mlp_first[0], mlp_second[0], mlp_master[0])
    qkv_full = after(qkv_full, *mlp_state)

    def images_of(array, start):
        return lax.dynamic_slice_in_dim(array, start * per_out, per_out, 0)

    own_index = head_pos * 2 + tensor_pos
    pair_index = (1 - head_pos) * 2 + tensor_pos
    attn_tokens = jnp.concatenate([images_of(tokens, own_index), images_of(tokens, pair_index)])
    attn_tokens = attn_tokens.reshape(2 * own_rows, features)
    own_kept = images_of(kept_counts, own_index)
    attn_kept = jnp.concatenate([own_kept, images_of(kept_counts, pair_index)])
    mlp_kept = jnp.concatenate([own_kept, images_of(kept_counts, head_pos * 2 + 1 - tensor_pos)])
    mlp_cot = jnp.concatenate([images_of(cotangent, tensor_pos), images_of(cotangent, 1 - tensor_pos)])
    positions = jnp.arange(slot_count, dtype=jnp.int32)
    mlp_valid = positions[None, :] < (BUF + mlp_kept)[:, None]
    mlp_cot = jnp.where(mlp_valid[:, :, None], mlp_cot, jnp.zeros_like(mlp_cot))
    mlp_cot = mlp_cot.reshape(2 * own_rows, features)
    own_valid = mlp_valid[:per_out].reshape(own_rows, 1).astype(F32)
    own_cot = mlp_cot[:own_rows].astype(F32)

    normed_one, inv_one = norm_parts(attn_tokens.astype(F32))
    low_one = (normed_one * ln1_gain + ln1_bias).astype(BF16)
    projected = dot(low_one, qkv_full, (1, 0)).astype(BF16)
    heads_out = attn_forward(attn_kept, projected, slot_count)
    pair_branch = dot(heads_out[own_rows:], out_full_t, (1, 1)).astype(BF16)
    branch_in = swap(pair_branch, HEAD)
    own_branch = dot(heads_out[:own_rows], out_full_t, (1, 1))
    residual = attn_tokens[:own_rows].astype(F32) + (own_branch + branch_in.astype(F32)) + out_bias
    normed_two, inv_two = norm_parts(residual)
    low_two = (normed_two * ln2_gain + ln2_bias).astype(BF16)

    low_in = swap(low_two, TENSOR)
    mlp_mine = after(mlp_mine, low_two)
    mlp_other = swap(mlp_mine, HEAD)
    flag = head_pos.reshape(1).astype(jnp.int32)
    up_local = lax.dynamic_slice_in_dim(up_bias, tensor_pos * hidden_cols, hidden_cols, 0)[None]
    hidden, grad_pre, own_sum, own_grad_normed = feed(
        flag, low_two, mlp_cot, mlp_mine, mlp_other, up_local, 0, (), 512, F32
    )
    hidden, grad_pre, pair_sum, pair_normed = feed(
        flag, low_in, mlp_cot, mlp_mine, mlp_other, up_local, 1, (hidden, grad_pre), 512, BF16
    )
    normed_in = swap(pair_normed, TENSOR)
    up_bias_part = pair_sum + own_sum
    normed_rows = jnp.concatenate([low_two, low_in])
    up_grad = dot(normed_rows, grad_pre, (0, 0)).astype(BF16)
    down_grad = dot(hidden, mlp_cot, (0, 0)).astype(BF16)
    mlp_owners = lax.axis_size((SHARD, HEAD))
    mlp_cap = mlp_master.shape[1]
    mlp_slots = slot_numbers(mlp_owner[0, :, 0], mlp_cap, mlp_owners)
    mlp_parts = mlp_parcel(mlp_slots, mlp_owners * mlp_cap, up_grad, down_grad)
    mlp_sum = lax.psum_scatter(mlp_parts, (SHARD, HEAD), scatter_dimension=0, tiled=True)
    resid_from, ln2_gain_part, ln2_bias_part = norm_back(
        own_grad_normed + normed_in.astype(F32), normed_two, inv_two, ln2_gain
    )
    down_bias_part = jnp.sum(own_cot, axis=0)
    grad_resid = own_cot + resid_from
    grad_branch = grad_resid.astype(BF16)
    out_bias_part = jnp.sum(grad_branch.astype(F32), axis=0)

    branch_rows = jnp.concatenate([grad_branch, after(swap(grad_branch, HEAD), mlp_parts)])
    grad_heads = dot(branch_rows, out_full_t, (1, 0)).astype(BF16)
    grad_proj = attn_backward(attn_kept, projected, grad_heads, slot_count)
    out_grad = dot(heads_out, branch_rows, (0, 0)).astype(BF16)
    qkv_grad = dot(low_one, grad_proj, (0, 0)).astype(BF16)
    pair_input = dot(grad_proj[own_rows:], qkv_full, (1, 1)).astype(BF16)
    input_in = swap(pair_input, HEAD)
    own_input = lax.optimization_barrier(dot(grad_proj[:own_rows], qkv_full, (1, 1)))
    tokens_from, ln1_gain_part, ln1_bias_part = norm_back(
        own_input + input_in.astype(F32), normed_one[:own_rows], inv_one[:own_rows], ln1_gain
    )
    tokens_grad = grad_resid + tokens_from

    up_whole = lax.dynamic_update_slice_in_dim(
        jnp.zeros((FF,), F32), up_bias_part[0], tensor_pos * hidden_cols, 0
    )
    small = jnp.concatenate(
        [
            ln1_gain_part,
            ln1_bias_part,
            ln2_gain_part,
            ln2_bias_part,
            out_bias_part,
            down_bias_part,
            up_whole,
        ]
    ).reshape(-1, LANES)

    def mlp_output(pair_mlp):
        mlp_in = swap(pair_mlp, TENSOR)
        own_mlp = dot(hidden[:own_rows], down_full_t, (1, 1))
        mlp_out = own_mlp + mlp_in.astype(F32) + down_bias
        return (own_valid * (residual + mlp_out)).astype(BF16)

    hidden, down_full_t = lax.optimization_barrier(
        (hidden, jnp.where(head_pos == 0, mlp_other, mlp_mine), grad_proj)
    )[:2]
    pair_mlp = dot(hidden[own_rows:], down_full_t, (1, 1)).astype(BF16)

    place = shard_pos.reshape(1).astype(jnp.int32)
    rows = features // BS

    shards = lax.axis_size(SHARD)
    tensors = lax.axis_size(TENSOR)
    attn_owners = shards * tensors
    attn_cap = attn_master.shape[1]
    attn_total = attn_owners * attn_cap
    attn_slots = slot_numbers(attn_owner[0, :, 0], attn_cap, attn_owners)
    direct = shards == 8 and tensors == 2
    if direct:
        owner = attn_owner[0, :, 0]
        inner = attn_slots - owner * attn_cap
        off_tensor = (owner % tensors) ^ tensor_pos
        off_shard = (owner // tensors) ^ shard_pos
        bit, high = off_shard % 2, off_shard // 2
        columns = shards // 2
        sizes = ((attn_cap + 1) // 2, attn_cap // 2)
        start = attn_owners * sizes[0]
        spot = jnp.where(
            inner < sizes[0],
            ((off_tensor * 2 + bit) * columns + high) * sizes[0] + inner,
            start + ((bit * 2 + off_tensor) * columns + high) * sizes[1] + inner - sizes[0],
        )
        parts = attn_parcel(spot, attn_total, qkv_grad, out_grad)

        def so_far(which, begin, count, arrived):
            total = parts[which * start + begin : which * start + begin + count].astype(F32)
            for array in arrived:
                total = total + array[begin : begin + count].astype(F32)
            return total

        spans = [columns * size for size in sizes]
        first_a = swap(parts[2 * spans[0] : 4 * spans[0]], TENSOR)
        first_b = across(parts[start + 2 * spans[1] : start + 4 * spans[1]], 1)
        next_a = so_far(0, spans[0], spans[0], (first_a,)).astype(BF16)
        next_b = so_far(1, spans[1], spans[1], (first_b,)).astype(BF16)
        second_a = across(next_a, 1)
        second_b = swap(next_b, TENSOR)
        second_a = after(second_a, tokens_grad)
        sums = [
            jnp.concatenate(
                [
                    so_far(0, step * sizes[0], sizes[0], (first_a, second_a)),
                    so_far(1, step * sizes[1], sizes[1], (first_b, second_b)),
                ]
            )
            for step in range(columns)
        ]
        arrived = []
        for step in range(1, columns):
            arrived.append(across(sums[step].astype(BF16), 2 * step))
        pair_mlp = after(pair_mlp, *sums)
        mlp_sum = after(mlp_sum, *sums)
    else:
        parts = attn_parcel(attn_slots, attn_total, qkv_grad, out_grad)
        attn_sum = lax.psum_scatter(parts, (SHARD, TENSOR), scatter_dimension=0, tiled=True)
        attn_sum = unpack(attn_sum).astype(F32)

    mlp_sum = unpack(mlp_sum).astype(F32)
    mlp_first_new, mlp_second_new, mlp_master_new = soap_update(mlp_sum, *mlp_state)
    mlp_dense = pack(mlp_master_new.astype(BF16))
    mlp_all = lax.all_gather(mlp_dense, (SHARD, HEAD), axis=0, tiled=True)

    if direct:
        arrived = lax.optimization_barrier((*arrived, mlp_dense))[:-1]
        attn_sum = add_up(sums[0], arrived)
    out = mlp_output(pair_mlp)
    attn_first_new, attn_second_new, attn_master_new = soap_update(
        attn_sum, attn_left[0], attn_right[0], attn_first[0], attn_second[0], attn_master[0]
    )
    attn_dense = pack(attn_master_new.astype(BF16))
    mlp_news = settle(mlp_sum, mlp_first_new, mlp_second_new, mlp_master_new)
    mlp_news = lax.optimization_barrier((*mlp_news, attn_dense))[:-1]
    mlp_outs = settle(*(jnp.transpose(a, (1, 2, 0)) for a in mlp_news))
    small = after(small, attn_dense)
    small = small + swap(small, HEAD)
    small = small + swap(small, TENSOR)

    own = w_qkv.shape[1]
    if direct:
        column = [attn_dense]
        for step in range(1, columns):
            column.append(across(attn_dense, 2 * step))
        empty = jnp.zeros((1,) + attn_dense.shape[1:], BF16)
        here = (off_tensor == 0) & (bit == 0)
        where = jnp.where(here, high * attn_cap + inner, columns * attn_cap)
        lists = [local_blocks(p, rows, group_cols // BS, own // BS) for p in (shard_pos, shard_pos ^ 1)]
        table = jnp.take(where, jnp.concatenate(lists), axis=0)
        table = after(table, *mlp_outs, small, out, tokens_grad)
        mine, theirs = pick(table, jnp.concatenate(column + [empty]), 2)
        small = after(small, theirs)
        small = small + across(small, 2)
        small = small + across(small, 4)
        mine = after(mine + across(theirs, 1), small)
        small = small + across(small, 1)
        w_qkv_new, w_out_new = attn_finish(
            after(mine, small), swap(mine, TENSOR), (w_qkv.shape, w_out.shape)
        )
        w_up_new, w_down_new = from_slots(
            partial(mlp_return_body, rows, hidden_cols // BS),
            mlp_slots,
            place,
            mlp_all,
            (w_up.shape, w_down.shape),
        )
    else:
        bit = 1
        while bit < shards:
            small = small + across(small, bit)
            bit *= 2
        attn_all = lax.all_gather(attn_dense, (SHARD, TENSOR), axis=0, tiled=True)
        attn_new = unpack(jnp.take(attn_all, attn_slots, axis=0))
        qkv_count = 3 * rows * (group_cols // BS)
        new_qkv = join_blocks(attn_new[:qkv_count], (3,), features, group_cols)
        new_out = join_blocks(attn_new[qkv_count:], (), group_cols, features)
        w_qkv_new = lax.dynamic_slice_in_dim(new_qkv, shard_pos * own, own, 1)
        w_out_new = lax.dynamic_slice_in_dim(new_out, shard_pos * own, own, 1)
        mlp_new = unpack(jnp.take(mlp_all, mlp_slots, axis=0))
        up_count = rows * (hidden_cols // BS)
        new_up = join_blocks(mlp_new[:up_count], (), features, hidden_cols)
        new_down = join_blocks(mlp_new[up_count:], (), hidden_cols, features)
        w_up_new = lax.dynamic_slice_in_dim(new_up, shard_pos * own, own, 0)
        w_down_new = lax.dynamic_slice_in_dim(new_down, shard_pos * own, own, 1)

    small = small.reshape(-1)
    small_sums = [small[i * features : (i + 1) * features] for i in range(6)] + [small[6 * features :]]

    return (
        out.reshape(per_out, slot_count, features),
        tokens_grad.reshape(per_out, slot_count, features),
        *small_sums,
        attn_sum[None],
        attn_first_new[None],
        attn_second_new[None],
        attn_master_new[None],
        *(jnp.transpose(array, (2, 0, 1))[None] for array in mlp_outs),
        w_qkv_new,
        w_out_new,
        w_up_new,
        w_down_new,
    )


def solution(mesh):
    placed = (
        P(SHARD, None, None),
        P(SHARD),
        P((SHARD, HEAD), None, None),
        P(None, SHARD, HEAD),
        P(HEAD, SHARD),
        P(SHARD, TENSOR),
        P(TENSOR, SHARD),
        P(),
        P(),
        P(),
        P(),
        P(),
        P(),
        P(),
        P(HEAD, None, None),
        P(TENSOR, None, None),
        P(HEAD, (SHARD, TENSOR), None, None),
        P(HEAD, (SHARD, TENSOR), None, None),
        P(HEAD, (SHARD, TENSOR), None, None),
        P(HEAD, (SHARD, TENSOR), None, None),
        P(HEAD, (SHARD, TENSOR), None, None),
        P(TENSOR, (SHARD, HEAD), None, None),
        P(TENSOR, (SHARD, HEAD), None, None),
        P(TENSOR, (SHARD, HEAD), None, None),
        P(TENSOR, (SHARD, HEAD), None, None),
        P(TENSOR, (SHARD, HEAD), None, None),
    )
    return jax.shard_map(
        per_device,
        mesh=mesh,
        in_specs=placed,
        out_specs=(
            P((SHARD, HEAD, TENSOR), None, None),
            P((SHARD, HEAD, TENSOR), None, None),
            P(),
            P(),
            P(),
            P(),
            P(),
            P(),
            P(),
            P(HEAD, (SHARD, TENSOR), None, None),
            P(HEAD, (SHARD, TENSOR), None, None),
            P(HEAD, (SHARD, TENSOR), None, None),
            P(HEAD, (SHARD, TENSOR), None, None),
            P(TENSOR, (SHARD, HEAD), None, None),
            P(TENSOR, (SHARD, HEAD), None, None),
            P(TENSOR, (SHARD, HEAD), None, None),
            P(TENSOR, (SHARD, HEAD), None, None),
            P(None, SHARD, HEAD),
            P(HEAD, SHARD),
            P(SHARD, TENSOR),
            P(TENSOR, SHARD),
        ),
        check_vma=False,
    )
```

```python
from functools import partial

import jax
import jax.numpy as jnp
from jax import lax
from jax.experimental import pallas as pl
from jax.experimental.pallas import tpu as pltpu
from jax.sharding import PartitionSpec as P


HD = 64
FF = 4096
BUF = 64
BS = 64
LANES = 128
SHARD, HEAD, TENSOR = "shard", "head", "tensor"
F32 = jnp.float32
BF16 = jnp.bfloat16

precise = lax.Precision.HIGH


def swap(value, axis):
    return lax.ppermute(value, axis, [(0, 1), (1, 0)])


def across(value, bits):
    size = lax.axis_size(SHARD)
    return lax.ppermute(value, SHARD, [(i, i ^ bits) for i in range(size)])


def settle(*arrays):
    anywhere = pl.BlockSpec(memory_space=pl.ANY)
    return pl.pallas_call(
        lambda *refs: None,
        out_shape=tuple(jax.ShapeDtypeStruct(a.shape, a.dtype) for a in arrays),
        in_specs=[anywhere] * len(arrays),
        out_specs=(anywhere,) * len(arrays),
        input_output_aliases={i: i for i in range(len(arrays))},
        name="settle",
    )(*arrays)


def dot(left, right, contract):
    return lax.dot_general(left, right, ((contract[:1], contract[1:]), ((), ())), preferred_element_type=F32)


def norm_parts(value):
    center = value - jnp.mean(value, axis=-1, keepdims=True)
    inv_root = lax.rsqrt(jnp.mean(center * center, axis=-1, keepdims=True) + 1e-06)
    return (center * inv_root, inv_root)


def norm_back(grad_out, normed, inv_root, gain_vec):
    grad_normed = grad_out * gain_vec
    first_mean = jnp.mean(grad_normed, axis=-1, keepdims=True)
    second_mean = jnp.mean(grad_normed * normed, axis=-1, keepdims=True)
    grad_in = inv_root * (grad_normed - first_mean - normed * second_mean)
    return (grad_in, jnp.sum(grad_out * normed, axis=0), jnp.sum(grad_out, axis=0))


def head_pair(rows, pair, which):
    groups = rows.shape[1] // (3 * HD)
    first = which * groups * HD + pair * LANES
    return rows[:, first : first + LANES]


def one_head_each(both):
    first = lax.broadcasted_iota(jnp.int32, both.shape, 0) < HD
    nothing = jnp.zeros_like(both)
    return (jnp.where(first, both, nothing), jnp.where(first, nothing, both))


def scaled(rows, pair):
    return head_pair(rows, pair, 0) * jnp.asarray(0.125, BF16)


def weights_of(scores, valid):
    scores = jnp.where(valid, scores, -1000000000.0)
    raised = jnp.exp(scores - jnp.max(scores, axis=0, keepdims=True))
    return (raised, 1.0 / jnp.sum(raised, axis=0, keepdims=True))


def key_mask(rows, count):
    slots = rows.shape[0]
    return lax.broadcasted_iota(jnp.int32, (slots, slots), 0) < BUF + count


def products(left, right):
    return [dot(left, one, (1, 0)) for one in one_head_each(right.T)]


def attn_forward_body(kept, rows, out):
    valid = key_mask(rows, kept[pl.program_id(0)])
    pairs = rows.shape[1] // (6 * HD)

    def scores_of(pair):
        return products(head_pair(rows, pair, 1), scaled(rows, pair))

    ahead = scores_of(0)
    for pair in range(pairs):
        scores = ahead
        if pair + 1 < pairs:
            ahead = scores_of(pair + 1)
        values = head_pair(rows, pair, 2).T
        halves = []
        for number in range(2):
            raised, scale = weights_of(scores[number], valid)
            value = values[number * HD : (number + 1) * HD]
            halves.append(dot(value, raised.astype(BF16), (1, 0)) * scale)
        out[:, pair * LANES : (pair + 1) * LANES] = jnp.concatenate(halves).T.astype(BF16)


def attn_forward(kept, rows, slots):
    images = kept.shape[0]
    width = rows.shape[1]
    return pl.pallas_call(
        attn_forward_body,
        out_shape=jax.ShapeDtypeStruct((images * slots, width // 3), BF16),
        grid_spec=pltpu.PrefetchScalarGridSpec(
            num_scalar_prefetch=1,
            grid=(images,),
            in_specs=[pl.BlockSpec((slots, width), lambda i, kept: (i, 0))],
            out_specs=pl.BlockSpec((slots, width // 3), lambda i, kept: (i, 0)),
        ),
        name="attn_forward",
    )(kept, rows)


def attn_backward_body(kept, rows, grads, out):
    valid = key_mask(rows, kept[pl.program_id(0)])
    width = rows.shape[1] // 3
    pairs = width // LANES
    first = lax.broadcasted_iota(jnp.int32, (rows.shape[0], LANES), 1) < HD

    def ahead_of(pair):
        grad = grads[:, pair * LANES : (pair + 1) * LANES]
        scores = products(head_pair(rows, pair, 1), scaled(rows, pair))
        return (scores, products(head_pair(rows, pair, 2), grad))

    ahead = ahead_of(0)
    for pair in range(pairs):
        scores, grad_probs = ahead
        if pair + 1 < pairs:
            ahead = ahead_of(pair + 1)
        window = slice(pair * LANES, (pair + 1) * LANES)
        probs = []
        grad_scores = []
        for number in range(2):
            raised, scale = weights_of(scores[number], valid)
            inner = jnp.sum(raised * grad_probs[number], axis=0, keepdims=True) * scale
            weights = raised * scale
            probs.append(weights.astype(BF16))
            grad_scores.append((weights * (grad_probs[number] - inner)).astype(BF16))
        keys_t = head_pair(rows, pair, 1).T
        parts = [dot(keys_t[n * HD : (n + 1) * HD], grad_scores[n], (1, 0)) for n in range(2)]
        out[:, window] = (jnp.concatenate(parts).T * 0.125).astype(BF16)
        for which, lefts, right in ((1, grad_scores, scaled(rows, pair)), (2, probs, grads[:, window])):
            start = which * width + pair * LANES
            parts = [dot(left, right, (1, 0)) for left in lefts]
            out[:, start : start + LANES] = jnp.where(first, *parts).astype(BF16)


def attn_backward(kept, rows, grads, slots):
    images = kept.shape[0]
    width = rows.shape[1]
    return pl.pallas_call(
        attn_backward_body,
        out_shape=jax.ShapeDtypeStruct(rows.shape, BF16),
        grid_spec=pltpu.PrefetchScalarGridSpec(
            num_scalar_prefetch=1,
            grid=(images,),
            in_specs=[
                pl.BlockSpec((slots, width), lambda i, kept: (i, 0)),
                pl.BlockSpec((slots, width // 3), lambda i, kept: (i, 0)),
            ],
            out_specs=pl.BlockSpec((slots, width), lambda i, kept: (i, 0)),
        ),
        name="attn_backward",
    )(kept, rows, grads)


ERF_TOP = (
    -2.72614225801306e-10,
    2.77068142495902e-08,
    -2.10102402082508e-06,
    -5.69250639462346e-05,
    -7.34990630326855e-04,
    -2.95459980854025e-03,
    -1.60960333262415e-02,
)
ERF_BOTTOM = (
    -1.45660718464996e-05,
    -2.13374055278905e-04,
    -1.68282697438203e-03,
    -7.37332916720468e-03,
    -1.42647390514189e-02,
)


def erf(value):
    value = jnp.clip(value, -4.0, 4.0)
    square = value * value
    top = jnp.full_like(value, ERF_TOP[0])
    for factor in ERF_TOP[1:]:
        top = top * square + factor
    bottom = jnp.full_like(value, ERF_BOTTOM[0])
    for factor in ERF_BOTTOM[1:]:
        bottom = bottom * square + factor
    return value * top / bottom


COL_CHUNK = 256


def feed_body(flag, rows, cot, mine, other, bias, *refs):
    hidden, grad_pre, bias_sum, grad_rows, up, down_t, total = refs[-7:]
    step = pl.program_id(0)
    for swapped in (False, True):

        @pl.when((flag[0] != 0) == swapped)
        def _():
            up[...] = other[...] if swapped else mine[...]
            down_t[...] = mine[...] if swapped else other[...]

    windows = [slice(start, start + COL_CHUNK) for start in range(0, up.shape[1], COL_CHUNK)]
    pairs = []
    for window in windows:
        pre = dot(rows[...], up[:, window], (1, 0)) + bias[:, window]
        pairs.append((pre, dot(cot[...], down_t[:, window], (1, 0))))
    for window, (pre, grad_hidden) in zip(windows, pairs):
        cdf = 0.5 + 0.5 * erf(pre * 0.7071067811865476)
        density = 0.3989422804014327 * jnp.exp(-0.5 * pre * pre)
        hidden[:, window] = (pre * cdf).astype(BF16)
        grad = (grad_hidden * (cdf + pre * density)).astype(BF16)
        grad_pre[:, window] = grad
        bias_sum[:, window] = jnp.sum(grad.astype(F32), axis=0, keepdims=True)
    part = dot(grad_pre[...], up[...], (1, 1))

    @pl.when(step == 0)
    def _():
        total[...] = part

    @pl.when(step > 0)
    def _():
        total[...] += part

    @pl.when(step == pl.num_programs(0) - 1)
    def _():
        grad_rows[...] = total[...].astype(grad_rows.dtype)


def feed(flag, rows, cot, mine, other, bias, half, held, col_block, grad_type):
    count, features = rows.shape
    width = mine.shape[1]
    whole = jax.ShapeDtypeStruct((2 * count, width), BF16)
    big = pl.BlockSpec((count, col_block), lambda j: (half, j))
    weight = pl.BlockSpec((features, col_block), lambda j: (0, j))
    line = pl.BlockSpec((1, col_block), lambda j: (0, j))
    passed = [pl.BlockSpec(memory_space=pl.ANY) for _ in held]
    return pl.pallas_call(
        feed_body,
        out_shape=(
            whole,
            whole,
            jax.ShapeDtypeStruct((1, width), F32),
            jax.ShapeDtypeStruct((count, features), grad_type),
        ),
        grid=(width // col_block,),
        in_specs=[
            pl.BlockSpec(memory_space=pltpu.SMEM),
            pl.BlockSpec((count, features), lambda j: (0, 0)),
            pl.BlockSpec((count, features), lambda j: (half, 0)),
            weight,
            weight,
            line,
            *passed,
        ],
        out_specs=(big, big, line, pl.BlockSpec((count, features), lambda j: (0, 0))),
        scratch_shapes=[
            pltpu.VMEM((features, col_block), BF16),
            pltpu.VMEM((features, col_block), BF16),
            pltpu.VMEM((count, features), F32),
        ],
        input_output_aliases={6: 0, 7: 1} if held else {},
        name="feed",
    )(flag, rows, cot, mine, other, bias, *held)


def slot_numbers(owner_list, capacity, owners):
    count = owner_list.shape[0]
    onehot = (owner_list[:, None] == jnp.arange(owners, dtype=jnp.int32)[None, :]).astype(BF16)
    order = jnp.arange(count, dtype=jnp.int32)
    before = (order[:, None] > order[None, :]).astype(BF16)
    earlier = dot(before, onehot, (1, 0))
    return owner_list * capacity + jnp.sum(earlier * onehot.astype(F32), axis=1).astype(jnp.int32)


def low_lanes():
    return lax.broadcasted_iota(jnp.int32, (BS // 2, LANES), 1) < BS


def to_parcel_body(indices_of, slots, *refs):
    *inputs, out = refs
    step = pl.program_id(0)

    @pl.when(step == 0)
    def _():
        out[...] = jnp.zeros(out.shape, out.dtype)

    low = low_lanes()
    for number, source in enumerate(inputs):
        rows, cols = source.shape
        for row in range(rows // BS):
            for pair in range(cols // LANES):
                window = pl.ds(pair * LANES, LANES)
                top = source[pl.ds(row * BS, BS // 2), window]
                bottom = source[pl.ds(row * BS + BS // 2, BS // 2), window]
                left, right = indices_of(number, step, row, pair)
                out[slots[left]] = jnp.where(low, top, pltpu.roll(bottom, BS, 1))
                out[slots[right]] = jnp.where(low, pltpu.roll(top, BS, 1), bottom)


def after(value, *others):
    return lax.optimization_barrier((value, *others))[0]


def to_parcel(slots, total, sources, indices_of):
    return pl.pallas_call(
        partial(to_parcel_body, indices_of),
        out_shape=jax.ShapeDtypeStruct((total, BS // 2, LANES), BF16),
        grid_spec=pltpu.PrefetchScalarGridSpec(
            num_scalar_prefetch=1,
            grid=(PARCEL_STEPS,),
            in_specs=[
                pl.BlockSpec((a.shape[0] // PARCEL_STEPS, a.shape[1]), lambda i, slots: (i, 0))
                for a in sources
            ],
            out_specs=pl.BlockSpec(
                (total, BS // 2, LANES), lambda i, slots: (0, 0, 0), pipeline_mode=pl.Buffered(1)
            ),
        ),
        name="to_parcel",
    )(slots, *sources)


PARCEL_STEPS = 4


def attn_parcel(slots, total, qkv_grad, out_grad):
    rows = qkv_grad.shape[0] // BS
    cols = out_grad.shape[0] // BS

    def indices_of(number, step, row, pair):
        if number == 0:
            matrix, col = divmod(2 * pair, cols)
            first = matrix * rows * cols + (step * (rows // PARCEL_STEPS) + row) * cols + col
        else:
            first = 3 * rows * cols + (step * (cols // PARCEL_STEPS) + row) * rows + 2 * pair
        return (first, first + 1)

    sources = (qkv_grad, out_grad)
    return to_parcel(slots, total, sources, indices_of)


def mlp_parcel(slots, total, up_grad, down_grad):
    rows = up_grad.shape[0] // BS
    cols = up_grad.shape[1] // BS

    def indices_of(number, step, row, pair):
        if number == 0:
            first = (step * (rows // PARCEL_STEPS) + row) * cols + 2 * pair
        else:
            first = rows * cols + (step * (cols // PARCEL_STEPS) + row) * rows + 2 * pair
        return (first, first + 1)

    return to_parcel(slots, total, (up_grad, down_grad), indices_of)


def pair_tile(left, right, low):
    top = jnp.where(low, left, pltpu.roll(right, BS, 1))
    bottom = jnp.where(low, pltpu.roll(left, BS, 1), right)
    return (top, bottom)


def local_blocks(place, rows, cols, own):
    matrix = jnp.arange(3, dtype=jnp.int32)[:, None, None]
    row = jnp.arange(own, dtype=jnp.int32)[None, :, None]
    col = jnp.arange(cols, dtype=jnp.int32)[None, None, :]
    first = ((matrix * rows + place * own + row) * cols + col).reshape(-1)
    row = jnp.arange(cols, dtype=jnp.int32)[:, None]
    col = jnp.arange(own, dtype=jnp.int32)[None, :]
    second = (3 * rows * cols + row * rows + place * own + col).reshape(-1)
    return jnp.concatenate([first, second])


def pick_body(table, held, *outs):
    count = outs[0].shape[0]
    for number, out in enumerate(outs):
        for block in range(count):
            out[block] = held[table[number * count + block]]


def pick(table, held, outs):
    whole = pl.BlockSpec(memory_space=pltpu.VMEM)
    shape = jax.ShapeDtypeStruct((table.shape[0] // outs,) + held.shape[1:], held.dtype)
    return pl.pallas_call(
        pick_body,
        out_shape=(shape,) * outs,
        in_specs=[pl.BlockSpec(memory_space=pltpu.SMEM), whole],
        out_specs=(whole,) * outs,
        name="pick",
    )(table, held)


def attn_finish_body(held, arrived, qkv_out, out_out):
    low = low_lanes()
    own = qkv_out.shape[1] // BS
    cols = qkv_out.shape[2] // BS

    def put(target, row, pair, first):
        top, bottom = pair_tile(held[first] + arrived[first], held[first + 1] + arrived[first + 1], low)
        window = pl.ds(pair * LANES, LANES)
        target[pl.ds(row * BS, BS // 2), window] = top
        target[pl.ds(row * BS + BS // 2, BS // 2), window] = bottom

    for matrix in range(3):
        for row in range(own):
            for pair in range(cols // 2):
                put(qkv_out.at[matrix], row, pair, (matrix * own + row) * cols + 2 * pair)
    for row in range(cols):
        for pair in range(own // 2):
            put(out_out, row, pair, 3 * own * cols + row * own + 2 * pair)


def attn_finish(held, arrived, shapes):
    whole = pl.BlockSpec(memory_space=pltpu.VMEM)
    return pl.pallas_call(
        attn_finish_body,
        out_shape=tuple(jax.ShapeDtypeStruct(shape, BF16) for shape in shapes),
        in_specs=[whole, whole],
        out_specs=tuple(whole for _ in shapes),
        name="attn_finish",
    )(held, arrived)


def mlp_return_body(rows, cols, slots, place, held, up_out, down_out):
    low = low_lanes()
    mine = place[0]
    own = up_out.shape[0] // BS

    def put(target, row, pair, first):
        top, bottom = pair_tile(held[slots[first]], held[slots[first + 1]], low)
        window = pl.ds(pair * LANES, LANES)
        target[pl.ds(row * BS, BS // 2), window] = top
        target[pl.ds(row * BS + BS // 2, BS // 2), window] = bottom

    for row in range(own):
        for pair in range(cols // 2):
            put(up_out, row, pair, (mine * own + row) * cols + 2 * pair)
    for row in range(cols):
        for pair in range(own // 2):
            put(down_out, row, pair, rows * cols + row * rows + mine * own + 2 * pair)


def from_slots(body, slots, place, held, shapes):
    whole = pl.BlockSpec(memory_space=pltpu.VMEM)
    table = pl.BlockSpec(memory_space=pltpu.SMEM)
    return pl.pallas_call(
        body,
        out_shape=tuple(jax.ShapeDtypeStruct(shape, BF16) for shape in shapes),
        in_specs=[table, table, whole],
        out_specs=tuple(whole for _ in shapes),
        name="from_slots",
    )(slots, place, held)


def add_up_body(*refs):
    *inputs, out = refs
    total = inputs[0][...].astype(F32)
    for source in inputs[1:]:
        total += source[...].astype(F32)
    out[:, : BS // 2, :] = total[:, :, :BS]
    out[:, BS // 2 :, :] = total[:, :, BS:]


def add_up(first, others):
    whole = pl.BlockSpec(memory_space=pltpu.VMEM)
    return pl.pallas_call(
        add_up_body,
        out_shape=jax.ShapeDtypeStruct((first.shape[0], BS, BS), F32),
        in_specs=[whole] * (1 + len(others)),
        out_specs=whole,
        name="add_up",
    )(first, *others)


def unpack(dense):
    return jnp.concatenate([dense[:, :, :BS], dense[:, :, BS:]], axis=1)


def pack(blocks):
    return jnp.concatenate([blocks[:, : BS // 2], blocks[:, BS // 2 :]], axis=2)


def join_blocks(blocks_in, leading, row_count, col_count):
    shaped = blocks_in.reshape(leading + (row_count // BS, col_count // BS, BS, BS))
    depth = len(leading)
    axes_order = tuple(range(depth)) + (depth, depth + 2, depth + 1, depth + 3)
    return shaped.transpose(axes_order).reshape(leading + (row_count, col_count))


def soap_update(gradient, left_basis, right_basis, first_moment, second, master):
    turned = jnp.einsum("sji,sjk->sik", left_basis, gradient, precision=precise)
    turned = jnp.einsum("sik,skl->sil", turned, right_basis, precision=precise)
    first_new = 0.95 * first_moment + 0.05 * turned
    second_new = 0.95 * second + 0.05 * turned * turned
    direction = first_new / (jnp.sqrt(second_new) + 1e-08)
    rotated_back = jnp.einsum("sij,sjk->sik", left_basis, direction, precision=precise)
    rotated_back = jnp.einsum("sik,slk->sil", rotated_back, right_basis, precision=precise)
    return (first_new, second_new, master - 0.05 * rotated_back)


def per_device(
    tokens,
    kept_counts,
    cotangent,
    w_qkv,
    w_out,
    w_up,
    w_down,
    ln1_gain,
    ln1_bias,
    ln2_gain,
    ln2_bias,
    out_bias,
    up_bias,
    down_bias,
    attn_owner,
    mlp_owner,
    attn_left,
    attn_right,
    attn_first,
    attn_second,
    attn_master,
    mlp_left,
    mlp_right,
    mlp_first,
    mlp_second,
    mlp_master,
):
    head_pos = lax.axis_index(HEAD)
    tensor_pos = lax.axis_index(TENSOR)
    shard_pos = lax.axis_index(SHARD)
    local_images, slot_count, features = tokens.shape
    per_out = local_images // 4
    own_rows = per_out * slot_count

    group_cols = w_qkv.shape[2]
    attn_mine = jnp.concatenate([w_qkv[0], w_qkv[1], w_qkv[2], w_out.T], axis=1)
    if lax.axis_size(TENSOR) == 2 and attn_mine.shape[0] % 32 == 0:
        half_rows = attn_mine.shape[0] // 2
        attn_half = lax.dynamic_slice_in_dim(attn_mine, tensor_pos * half_rows, half_rows, 0)
        attn_half = lax.all_gather(attn_half, SHARD, axis=0)
        first = tensor_pos == 0

        def both_halves(held):
            other = swap(held, TENSOR)
            parts = [jnp.where(first, held, other), jnp.where(first, other, held)]
            return jnp.stack(parts, axis=1).reshape(features, held.shape[2])

        qkv_full = both_halves(attn_half[:, :, : 3 * group_cols])
        out_full_t = both_halves(after(attn_half[:, :, 3 * group_cols :], qkv_full))
    else:
        attn_full = lax.all_gather(attn_mine, SHARD, axis=0, tiled=True)
        qkv_full = attn_full[:, : 3 * group_cols]
        out_full_t = attn_full[:, 3 * group_cols :]
    mlp_mine = lax.all_gather(
        after(jnp.where(head_pos == 0, w_up, w_down.T), attn_mine), SHARD, axis=0, tiled=True
    )
    hidden_cols = mlp_mine.shape[1]
    mlp_state = settle(mlp_left[0], mlp_right[0], mlp_first[0], mlp_second[0], mlp_master[0])
    qkv_full = after(qkv_full, *mlp_state)

    def images_of(array, start):
        return lax.dynamic_slice_in_dim(array, start * per_out, per_out, 0)

    own_index = head_pos * 2 + tensor_pos
    pair_index = (1 - head_pos) * 2 + tensor_pos
    attn_tokens = jnp.concatenate([images_of(tokens, own_index), images_of(tokens, pair_index)])
    attn_tokens = attn_tokens.reshape(2 * own_rows, features)
    own_kept = images_of(kept_counts, own_index)
    attn_kept = jnp.concatenate([own_kept, images_of(kept_counts, pair_index)])
    mlp_kept = jnp.concatenate([own_kept, images_of(kept_counts, head_pos * 2 + 1 - tensor_pos)])
    mlp_cot = jnp.concatenate([images_of(cotangent, tensor_pos), images_of(cotangent, 1 - tensor_pos)])
    positions = jnp.arange(slot_count, dtype=jnp.int32)
    mlp_valid = positions[None, :] < (BUF + mlp_kept)[:, None]
    mlp_cot = jnp.where(mlp_valid[:, :, None], mlp_cot, jnp.zeros_like(mlp_cot))
    mlp_cot = mlp_cot.reshape(2 * own_rows, features)
    own_valid = mlp_valid[:per_out].reshape(own_rows, 1).astype(F32)
    own_cot = mlp_cot[:own_rows].astype(F32)

    normed_one, inv_one = norm_parts(attn_tokens.astype(F32))
    low_one = (normed_one * ln1_gain + ln1_bias).astype(BF16)
    projected = dot(low_one, qkv_full, (1, 0)).astype(BF16)
    heads_out = attn_forward(attn_kept, projected, slot_count)
    pair_branch = dot(heads_out[own_rows:], out_full_t, (1, 1)).astype(BF16)
    branch_in = swap(pair_branch, HEAD)
    own_branch = dot(heads_out[:own_rows], out_full_t, (1, 1))
    residual = attn_tokens[:own_rows].astype(F32) + (own_branch + branch_in.astype(F32)) + out_bias
    normed_two, inv_two = norm_parts(residual)
    low_two = (normed_two * ln2_gain + ln2_bias).astype(BF16)

    low_in = swap(low_two, TENSOR)
    mlp_mine = after(mlp_mine, low_two)
    mlp_other = swap(mlp_mine, HEAD)
    flag = head_pos.reshape(1).astype(jnp.int32)
    up_local = lax.dynamic_slice_in_dim(up_bias, tensor_pos * hidden_cols, hidden_cols, 0)[None]
    hidden, grad_pre, own_sum, own_grad_normed = feed(
        flag, low_two, mlp_cot, mlp_mine, mlp_other, up_local, 0, (), 512, F32
    )
    hidden, grad_pre, pair_sum, pair_normed = feed(
        flag, low_in, mlp_cot, mlp_mine, mlp_other, up_local, 1, (hidden, grad_pre), 512, BF16
    )
    normed_in = swap(pair_normed, TENSOR)
    up_bias_part = pair_sum + own_sum
    normed_rows = jnp.concatenate([low_two, low_in])
    up_grad = dot(normed_rows, grad_pre, (0, 0)).astype(BF16)
    down_grad = dot(hidden, mlp_cot, (0, 0)).astype(BF16)
    mlp_owners = lax.axis_size((SHARD, HEAD))
    mlp_cap = mlp_master.shape[1]
    mlp_slots = slot_numbers(mlp_owner[0, :, 0], mlp_cap, mlp_owners)
    mlp_parts = mlp_parcel(mlp_slots, mlp_owners * mlp_cap, up_grad, down_grad)
    mlp_sum = lax.psum_scatter(mlp_parts, (SHARD, HEAD), scatter_dimension=0, tiled=True)
    resid_from, ln2_gain_part, ln2_bias_part = norm_back(
        own_grad_normed + normed_in.astype(F32), normed_two, inv_two, ln2_gain
    )
    down_bias_part = jnp.sum(own_cot, axis=0)
    grad_resid = own_cot + resid_from
    grad_branch = grad_resid.astype(BF16)
    out_bias_part = jnp.sum(grad_branch.astype(F32), axis=0)

    branch_rows = jnp.concatenate([grad_branch, after(swap(grad_branch, HEAD), mlp_parts)])
    grad_heads = dot(branch_rows, out_full_t, (1, 0)).astype(BF16)
    grad_proj = attn_backward(attn_kept, projected, grad_heads, slot_count)
    out_grad = dot(heads_out, branch_rows, (0, 0)).astype(BF16)
    qkv_grad = dot(low_one, grad_proj, (0, 0)).astype(BF16)
    pair_input = dot(grad_proj[own_rows:], qkv_full, (1, 1)).astype(BF16)
    input_in = swap(pair_input, HEAD)
    own_input = lax.optimization_barrier(dot(grad_proj[:own_rows], qkv_full, (1, 1)))
    tokens_from, ln1_gain_part, ln1_bias_part = norm_back(
        own_input + input_in.astype(F32), normed_one[:own_rows], inv_one[:own_rows], ln1_gain
    )
    tokens_grad = grad_resid + tokens_from

    up_whole = lax.dynamic_update_slice_in_dim(
        jnp.zeros((FF,), F32), up_bias_part[0], tensor_pos * hidden_cols, 0
    )
    small = jnp.concatenate(
        [
            ln1_gain_part,
            ln1_bias_part,
            ln2_gain_part,
            ln2_bias_part,
            out_bias_part,
            down_bias_part,
            up_whole,
        ]
    ).reshape(-1, LANES)

    def mlp_output(pair_mlp):
        mlp_in = swap(pair_mlp, TENSOR)
        own_mlp = dot(hidden[:own_rows], down_full_t, (1, 1))
        mlp_out = own_mlp + mlp_in.astype(F32) + down_bias
        return (own_valid * (residual + mlp_out)).astype(BF16)

    hidden, down_full_t = lax.optimization_barrier(
        (hidden, jnp.where(head_pos == 0, mlp_other, mlp_mine), grad_proj)
    )[:2]
    pair_mlp = dot(hidden[own_rows:], down_full_t, (1, 1)).astype(BF16)

    place = shard_pos.reshape(1).astype(jnp.int32)
    rows = features // BS

    shards = lax.axis_size(SHARD)
    tensors = lax.axis_size(TENSOR)
    attn_owners = shards * tensors
    attn_cap = attn_master.shape[1]
    attn_total = attn_owners * attn_cap
    attn_slots = slot_numbers(attn_owner[0, :, 0], attn_cap, attn_owners)
    direct = shards == 8 and tensors == 2
    if direct:
        owner = attn_owner[0, :, 0]
        inner = attn_slots - owner * attn_cap
        off_tensor = (owner % tensors) ^ tensor_pos
        off_shard = (owner // tensors) ^ shard_pos
        bit, high = off_shard % 2, off_shard // 2
        columns = shards // 2
        sizes = ((attn_cap + 1) // 2, attn_cap // 2)
        start = attn_owners * sizes[0]
        spot = jnp.where(
            inner < sizes[0],
            ((off_tensor * 2 + bit) * columns + high) * sizes[0] + inner,
            start + ((bit * 2 + off_tensor) * columns + high) * sizes[1] + inner - sizes[0],
        )
        parts = attn_parcel(spot, attn_total, qkv_grad, out_grad)

        def so_far(which, begin, count, arrived):
            total = parts[which * start + begin : which * start + begin + count].astype(F32)
            for array in arrived:
                total = total + array[begin : begin + count].astype(F32)
            return total

        spans = [columns * size for size in sizes]
        first_a = swap(parts[2 * spans[0] : 4 * spans[0]], TENSOR)
        first_b = across(parts[start + 2 * spans[1] : start + 4 * spans[1]], 1)
        next_a = so_far(0, spans[0], spans[0], (first_a,)).astype(BF16)
        next_b = so_far(1, spans[1], spans[1], (first_b,)).astype(BF16)
        second_a = across(next_a, 1)
        second_b = swap(next_b, TENSOR)
        second_a = after(second_a, tokens_grad)
        sums = [
            jnp.concatenate(
                [
                    so_far(0, step * sizes[0], sizes[0], (first_a, second_a)),
                    so_far(1, step * sizes[1], sizes[1], (first_b, second_b)),
                ]
            )
            for step in range(columns)
        ]
        arrived = []
        for step in range(1, columns):
            arrived.append(across(sums[step].astype(BF16), 2 * step))
        pair_mlp = after(pair_mlp, *sums)
        mlp_sum = after(mlp_sum, *sums)
    else:
        parts = attn_parcel(attn_slots, attn_total, qkv_grad, out_grad)
        attn_sum = lax.psum_scatter(parts, (SHARD, TENSOR), scatter_dimension=0, tiled=True)
        attn_sum = unpack(attn_sum).astype(F32)

    mlp_sum = unpack(mlp_sum).astype(F32)
    mlp_first_new, mlp_second_new, mlp_master_new = soap_update(mlp_sum, *mlp_state)
    mlp_dense = pack(mlp_master_new.astype(BF16))
    mlp_all = lax.all_gather(mlp_dense, (SHARD, HEAD), axis=0, tiled=True)

    if direct:
        arrived = lax.optimization_barrier((*arrived, mlp_dense))[:-1]
        attn_sum = add_up(sums[0], arrived)
    out = mlp_output(pair_mlp)
    attn_first_new, attn_second_new, attn_master_new = soap_update(
        attn_sum, attn_left[0], attn_right[0], attn_first[0], attn_second[0], attn_master[0]
    )
    attn_dense = pack(attn_master_new.astype(BF16))
    mlp_news = settle(mlp_sum, mlp_first_new, mlp_second_new, mlp_master_new)
    mlp_news = lax.optimization_barrier((*mlp_news, attn_dense))[:-1]
    mlp_outs = settle(*(jnp.transpose(a, (1, 2, 0)) for a in mlp_news))
    small = after(small, attn_dense)
    small = small + swap(small, HEAD)

    own = w_qkv.shape[1]
    if direct:
        column = [attn_dense]
        for step in range(1, columns):
            column.append(across(attn_dense, 2 * step))
        empty = jnp.zeros((1,) + attn_dense.shape[1:], BF16)
        here = (off_tensor == 0) & (bit == 0)
        where = jnp.where(here, high * attn_cap + inner, columns * attn_cap)
        lists = [local_blocks(p, rows, group_cols // BS, own // BS) for p in (shard_pos, shard_pos ^ 1)]
        table = jnp.take(where, jnp.concatenate(lists), axis=0)
        small = small + swap(small, TENSOR)
        table = after(table, *mlp_outs, small, out)
        mine, theirs = pick(table, jnp.concatenate(column + [empty]), 2)
        small = after(small, theirs)
        small = small + across(small, 2)
        small = small + across(small, 4)
        mine = after(mine + across(theirs, 1), small)
        small = small + across(small, 1)
        w_qkv_new, w_out_new = attn_finish(
            after(mine, small), swap(mine, TENSOR), (w_qkv.shape, w_out.shape)
        )
        w_up_new, w_down_new = from_slots(
            partial(mlp_return_body, rows, hidden_cols // BS),
            mlp_slots,
            place,
            mlp_all,
            (w_up.shape, w_down.shape),
        )
    else:
        small = small + swap(small, TENSOR)
        bit = 1
        while bit < shards:
            small = small + across(small, bit)
            bit *= 2
        attn_all = lax.all_gather(attn_dense, (SHARD, TENSOR), axis=0, tiled=True)
        attn_new = unpack(jnp.take(attn_all, attn_slots, axis=0))
        qkv_count = 3 * rows * (group_cols // BS)
        new_qkv = join_blocks(attn_new[:qkv_count], (3,), features, group_cols)
        new_out = join_blocks(attn_new[qkv_count:], (), group_cols, features)
        w_qkv_new = lax.dynamic_slice_in_dim(new_qkv, shard_pos * own, own, 1)
        w_out_new = lax.dynamic_slice_in_dim(new_out, shard_pos * own, own, 1)
        mlp_new = unpack(jnp.take(mlp_all, mlp_slots, axis=0))
        up_count = rows * (hidden_cols // BS)
        new_up = join_blocks(mlp_new[:up_count], (), features, hidden_cols)
        new_down = join_blocks(mlp_new[up_count:], (), hidden_cols, features)
        w_up_new = lax.dynamic_slice_in_dim(new_up, shard_pos * own, own, 0)
        w_down_new = lax.dynamic_slice_in_dim(new_down, shard_pos * own, own, 1)

    small = small.reshape(-1)
    small_sums = [small[i * features : (i + 1) * features] for i in range(6)] + [small[6 * features :]]

    return (
        out.reshape(per_out, slot_count, features),
        tokens_grad.reshape(per_out, slot_count, features),
        *small_sums,
        attn_sum[None],
        attn_first_new[None],
        attn_second_new[None],
        attn_master_new[None],
        *(jnp.transpose(array, (2, 0, 1))[None] for array in mlp_outs),
        w_qkv_new,
        w_out_new,
        w_up_new,
        w_down_new,
    )


def solution(mesh):
    placed = (
        P(SHARD, None, None),
        P(SHARD),
        P((SHARD, HEAD), None, None),
        P(None, SHARD, HEAD),
        P(HEAD, SHARD),
        P(SHARD, TENSOR),
        P(TENSOR, SHARD),
        P(),
        P(),
        P(),
        P(),
        P(),
        P(),
        P(),
        P(HEAD, None, None),
        P(TENSOR, None, None),
        P(HEAD, (SHARD, TENSOR), None, None),
        P(HEAD, (SHARD, TENSOR), None, None),
        P(HEAD, (SHARD, TENSOR), None, None),
        P(HEAD, (SHARD, TENSOR), None, None),
        P(HEAD, (SHARD, TENSOR), None, None),
        P(TENSOR, (SHARD, HEAD), None, None),
        P(TENSOR, (SHARD, HEAD), None, None),
        P(TENSOR, (SHARD, HEAD), None, None),
        P(TENSOR, (SHARD, HEAD), None, None),
        P(TENSOR, (SHARD, HEAD), None, None),
    )
    return jax.shard_map(
        per_device,
        mesh=mesh,
        in_specs=placed,
        out_specs=(
            P((SHARD, HEAD, TENSOR), None, None),
            P((SHARD, HEAD, TENSOR), None, None),
            P(),
            P(),
            P(),
            P(),
            P(),
            P(),
            P(),
            P(HEAD, (SHARD, TENSOR), None, None),
            P(HEAD, (SHARD, TENSOR), None, None),
            P(HEAD, (SHARD, TENSOR), None, None),
            P(HEAD, (SHARD, TENSOR), None, None),
            P(TENSOR, (SHARD, HEAD), None, None),
            P(TENSOR, (SHARD, HEAD), None, None),
            P(TENSOR, (SHARD, HEAD), None, None),
            P(TENSOR, (SHARD, HEAD), None, None),
            P(None, SHARD, HEAD),
            P(HEAD, SHARD),
            P(SHARD, TENSOR),
            P(TENSOR, SHARD),
        ),
        check_vma=False,
    )
```
